32 devices in a mesh: grp: 2 (over y), exp: 4 (over x, core), hid: 4 (over z).
Axes of the slice: x: 2, y: 2, z: 4, core: 2. Of those that a mesh axis runs over, the one named last changes fastest.
Arguments:
- tokens: bfloat16 [1024, 4096], P(('grp', 'exp'), 'hid'), parts along dimension 0, may hold values from -6 to 6
- grad_out: bfloat16 [1024, 4096], P(('grp', 'exp'), 'hid'), parts along dimension 0, may hold values from -3 to 3
- gates: bfloat16 [1024, 2], P(('grp', 'exp')), parts along dimension 0, may hold values from 0.049804688 to 1
- block_experts: int32 [8, 2], P('grp'), parts along dimension 0, may hold values from 0 to 3, all different within a row; in each aligned block of 4 rows (0 to 3, 4 to 7, ...) at most 2 rows name the same one
- w_gate: bfloat16 [4, 4096, 8192], P('exp', None, 'hid'), may hold values from -0.125 to 0.125
- w_up: bfloat16 [4, 4096, 8192], P('exp', None, 'hid'), may hold values from -0.125 to 0.125
- w_down: bfloat16 [4, 8192, 4096], P('exp', 'hid'), may hold values from -0.0625 to 0.0625
Outputs:
- d_tokens: bfloat16 [1024, 4096], P(('grp', 'exp'), 'hid'), parts along dimension 0
- d_gates: float32 [1024, 2], P(('grp', 'exp')), parts along dimension 0
The draws below stay inside these ranges and needn't reach their ends.
There are 2 independent parts, one for each index of `grp`. The reference program is written for one: setup_inputs(seed, part) draws one part's arguments, and reference() takes and returns one part's arrays. A program takes and returns all parts, laid end to end along the dimension named above; an argument that names none is the same for every part. Nothing has to cross between parts.
Inputs may be any that keep to these rules, and one draw needn't show every extreme that they name: `block_experts`: each row names two different experts for one block of 128 tokens; no expert is named by more than 2 of the 4 blocks, one expert by exactly 2, and every expert by some block.
All inputs are finite; a program needn't handle non-finite values.
Results may differ from the reference program's by a relative error of at most 0.0049.
Values may be sent and summed in bfloat16 or wider, within the bound.
A program may use at most 192 MiB of HBM per device.

```python
import math
import jax
import jax.numpy as jnp
import numpy as np
from jax import lax

D = 4096
FF = 8192
BLOCK = 128
EXPERTS = 4
TOKENS = 512
NBLK = 4
CAPB = 2


def raised(drawn, own_key, source, target, blocks, factor):
    owner, partner = [(jnp.arange(drawn.shape[position]) // (drawn.shape[position] // blocks)).reshape([-1 if axis == position else 1 for axis in range(drawn.ndim)]) for position in (source, target)]
    chosen = jax.random.permutation(own_key, blocks)[partner]
    strong = (owner == chosen) | (owner == (partner + blocks // 2) % blocks)
    return jnp.where(strong, factor * drawn, drawn)


def block_scale(key, shape, cuts, smallest, high):
    factor_of = 1.0
    for dim, blocks in cuts:
        steps = jax.random.uniform(jax.random.fold_in(jax.random.fold_in(key, 6), dim), (blocks,), jnp.float32, smallest / len(cuts), high / len(cuts))
        factor_of = factor_of * jnp.repeat(jnp.exp(steps), shape[dim] // blocks).reshape((-1,) + (1,) * (len(shape) - 1 - dim))
    return factor_of


def routed_block(stream_key, own, number, rows, number_of, top, most, lean):
    order = jax.random.permutation(stream_key, number_of)
    packed, common = portions_of(number_of, rows * top, most, lean, True), portions_of(number_of, rows * top, most, lean, False)
    places = jnp.arange(number_of)

    def named(sizes, rotation):
        used = int((sizes > 0).sum())
        fixed = max(1, used // 4)
        shifted = fixed + (places - fixed + rotation * (used - fixed)) % max(1, number_of - fixed)
        return jnp.zeros((number_of,), jnp.int32).at[order[jnp.where(places < fixed, places, shifted)]].set(jnp.asarray(sizes, jnp.int32))

    sizes = jnp.where(number % 4 == 0, named(packed, number // 4), named(common, number - number // 4 - 1))
    mixed = jax.random.permutation(jax.random.fold_in(own, 3), number_of)
    donor, receiver = mixed[0:number_of // 2 * 2:2], mixed[1:number_of // 2 * 2:2]
    margin = jnp.minimum(sizes[donor] - 1, most - sizes[receiver]) // 2
    margin = jnp.where((donor == order[0]) | (receiver == order[0]) | (sizes[receiver] == 0), 0, jnp.maximum(margin, 0))
    shifted = jax.random.randint(jax.random.fold_in(own, 4), (number_of // 2,), 0, 1 << 20) % (margin + 1)
    sizes = sizes.at[donor].add(-shifted).at[receiver].add(shifted)
    items = jnp.searchsorted(jnp.cumsum(sizes), jnp.arange(rows * top), side="right").astype(jnp.int32)
    grid = items.reshape(top, rows).T
    grid = grid[jax.random.permutation(jax.random.fold_in(own, 1), rows)]
    rotation = jax.random.randint(jax.random.fold_in(own, 2), (rows, 1), 0, top)
    return jnp.take_along_axis(grid, (jnp.arange(top)[None, :] + rotation) % top, axis=1)


def portions_of(number_of, total, limit, slope, full):
    loads = [(1 << 20) // math.isqrt(rank ** slope) + 1 for rank in range(1, number_of + 1)]
    largest = limit if full else min(limit, max(-(-total // number_of), total * loads[0] // sum(loads)))
    least = 1 if total - largest >= number_of - 1 else 0
    counts, surplus = [largest] + [least] * (number_of - 1), total - largest - least * (number_of - 1)
    while surplus > 0:
        candidates = [i for i in range(1, number_of) if counts[i] < largest] or [i for i in range(1, number_of) if counts[i] < limit]
        whole, left = sum([loads[i] for i in candidates]), surplus
        for i in candidates:
            more = min(limit - counts[i], max(1, left * loads[i] // whole), surplus)
            counts[i] = counts[i] + more
            surplus = surplus - more
    return np.array(counts)


def scatter_about(stream_key, extent, spread, bound, cuts=(), held_as=jnp.bfloat16):
    factor_of = block_scale(stream_key, extent, cuts, -0.22, 0.18) if cuts else 1.0
    values = jax.random.normal(stream_key, extent, jnp.float32) * spread * factor_of
    return jnp.minimum(jnp.maximum(values, -bound), bound).astype(held_as)


def heavy_noise(rng, shape, spread, limit, pieces, heavy, kind=jnp.bfloat16):
    entries = spread * jax.random.normal(rng, shape, jnp.float32)
    if pieces:
        entries = entries * block_scale(rng, shape, pieces, -0.22, 0.18)
    return jnp.clip(raised(entries, jax.random.fold_in(rng, 3), *heavy), -limit, limit).astype(kind)


def setup_inputs(seed: int = 0, part: int = 0) -> dict:
    key_list = jax.random.split(jax.random.key(seed), 8)
    part_splits = jax.random.split(jax.random.fold_in(key_list[7], part), 8)
    tokens = scatter_about(part_splits[0], (TOKENS, D), 1.0, 6.0, ((0, 4), (1, 4)))
    grad_out = scatter_about(part_splits[1], (TOKENS, D), 0.5, 3.0, ((0, 4), (1, 4)))
    gates = jnp.clip(0.049804688 + 0.9501953 * jax.random.uniform(part_splits[2], (TOKENS, 2), jnp.float32) ** block_scale(part_splits[2], (TOKENS, 2), ((0, 4),), -0.2, 0.2), 0.049804688, 1.0).astype(jnp.bfloat16)
    block_experts_keys = jax.random.split(jax.random.fold_in(part_splits[3], 1), NBLK // NBLK)
    block_experts_turns = jax.random.permutation(jax.random.fold_in(part_splits[3], 3), NBLK // NBLK)
    block_experts = jax.vmap(lambda own, number: routed_block(jax.random.fold_in(part_splits[3], 2), own, number, NBLK, EXPERTS, 2, CAPB, 2))(block_experts_keys, block_experts_turns).reshape((NBLK, 2))
    w_gate = heavy_noise(key_list[4], (EXPERTS, D, FF), D ** -0.5, 0.125, ((0, 4), (2, 4)), (2, 1, 4, 2.0))
    w_up = heavy_noise(key_list[5], (EXPERTS, D, FF), D ** -0.5, 0.125, ((0, 4), (2, 4)), (2, 1, 4, 2.0))
    w_down = scatter_about(key_list[6], (EXPERTS, FF, D), FF ** -0.5, 0.0625, ((0, 4), (1, 4)))
    return {"tokens": tokens, "grad_out": grad_out, "gates": gates, "block_experts": block_experts, "w_gate": w_gate, "w_up": w_up, "w_down": w_down}


def expert_pass(x_rows, dy_rows, gate_column, w_one, w_three, w_two):
    pre_gate = jnp.dot(x_rows, w_one, preferred_element_type=jnp.float32)
    pre_up = jnp.dot(x_rows, w_three, preferred_element_type=jnp.float32)
    d_hidden = jnp.dot(dy_rows, w_two.T, preferred_element_type=jnp.float32)
    sigmoid_gate = jax.nn.sigmoid(pre_gate)
    activated = pre_gate * sigmoid_gate
    score = jnp.sum(activated * pre_up * d_hidden, axis=1)
    scaled = gate_column[:, None] * d_hidden
    d_pre_gate = (scaled * pre_up * sigmoid_gate * (1.0 + pre_gate * (1.0 - sigmoid_gate))).astype(jnp.bfloat16)
    d_pre_up = (scaled * activated).astype(jnp.bfloat16)
    part = jnp.dot(d_pre_gate, w_one.T, preferred_element_type=jnp.float32)
    part = part + jnp.dot(d_pre_up, w_three.T, preferred_element_type=jnp.float32)
    return part, score


def reference(tokens, grad_out, gates, block_experts, w_gate, w_up, w_down):
    rows_x = tokens.reshape(NBLK, BLOCK, D)
    rows_dy = grad_out.reshape(NBLK, BLOCK, D)
    gate_rows = gates.astype(jnp.float32).reshape(NBLK, BLOCK, 2)

    def one_pair(pair_index):
        block_index = pair_index // 2
        slot_index = pair_index % 2
        expert = block_experts[block_index, slot_index]
        gate_column = jnp.take(gate_rows[block_index], slot_index, axis=1)
        return expert_pass(rows_x[block_index], rows_dy[block_index], gate_column,
                           w_gate[expert], w_up[expert], w_down[expert])

    parts, scores = lax.map(one_pair, jnp.arange(2 * NBLK, dtype=jnp.int32))
    parts = parts.reshape(NBLK, 2, BLOCK, D)
    d_tokens = (parts[:, 0] + parts[:, 1]).reshape(TOKENS, D).astype(jnp.bfloat16)
    d_gates = jnp.transpose(scores.reshape(NBLK, 2, BLOCK), (0, 2, 1)).reshape(TOKENS, 2)
    return d_tokens, d_gates
```

```python
import functools
import jax
import jax.numpy as jnp
from jax import lax
from jax.experimental import pallas as pl
from jax.experimental.pallas import tpu as pltpu
from jax.sharding import PartitionSpec as P

BLOCK = 128


HIGHEST = lax.Precision.HIGHEST
CONTRACT_LAST = (((1,), (1,)), ((), ()))
MESH = pl.DeviceIdType.MESH
TILE = 512


def passed_along(block, axis, distance):
    devices = range(lax.axis_size(axis))
    route = [((i - distance) % len(devices), i) for i in devices]
    return lax.ppermute(block, axis, route)


def routing(block_experts, own_index):
    blocks_all = block_experts.shape[0]
    capacity = blocks_all // 2
    matched = block_experts == own_index
    chosen = jnp.any(matched, axis=1)
    slot_of = matched[:, 1].astype(jnp.int32)
    position = jnp.cumsum(chosen.astype(jnp.int32)) - 1
    placed = (position[None, :] == jnp.arange(capacity, dtype=jnp.int32)[:, None]) & chosen[None, :]
    placed_int = placed.astype(jnp.int32)
    list_block = jnp.sum(placed_int * jnp.arange(blocks_all, dtype=jnp.int32)[None, :], axis=1)
    list_slot = jnp.sum(placed_int * slot_of[None, :], axis=1)
    live = jnp.any(placed, axis=1)
    return list_block, list_slot, live


def dispatch_kernel(nz, ne, tok, width, tok_ref, dy_ref, gate_ref, pick_ref, slot_ref, w1_ref, w3_ref, w2_ref,
                    dpg_ref, dpu_ref, score_ref,
                    xb, db, gb, w1, w3, w2, pg, pu, dh,
                    s_up, s_dn, s_x, s_c, rsem, gs, gr, wsem, lsem):
    z = lax.axis_index("hid")
    e = lax.axis_index("exp")
    mate = e + 1 - 2 * lax.rem(e, 2)
    across = lax.rem(e + 2, ne)
    bufs = (xb, db)
    hidden = w1.shape[2]

    def weights(q, slot):
        rows = pl.ds(pl.multiple_of(q * width, width), width)
        return (
            pltpu.make_async_copy(w1_ref.at[0, rows, :], w1.at[slot], wsem.at[slot, 0]),
            pltpu.make_async_copy(w3_ref.at[0, rows, :], w3.at[slot], wsem.at[slot, 1]),
            pltpu.make_async_copy(w2_ref.at[0, :, rows], w2.at[slot], wsem.at[slot, 2]),
        )

    def send(a, zq, eq, ssem, dev):
        return pltpu.make_async_remote_copy(
            src_ref=bufs[a].at[zq, eq], dst_ref=bufs[a].at[zq, eq],
            send_sem=ssem, recv_sem=rsem.at[a, zq, eq],
            device_id=dev, device_id_type=MESH)

    def up(a, zq):
        return send(a, zq, e, s_up.at[a, zq], {"hid": z + 1})

    def down(a, zq):
        return send(a, zq, e, s_dn.at[a, zq], {"hid": z - 1})

    def over_x(a, zq):
        return send(a, zq, e, s_x.at[a, zq], {"exp": across})

    def to_mate(a, zq, eq, k):
        return send(a, zq, eq, s_c.at[a, zq, k], {"exp": mate})

    def arrived(a, zq, eq):
        send(a, zq, eq, s_x.at[a, zq], {"exp": across}).wait_recv()

    def gate_send(eq, k, dev):
        return pltpu.make_async_remote_copy(
            src_ref=gb.at[eq], dst_ref=gb.at[eq], send_sem=gs.at[k], recv_sem=gr.at[eq],
            device_id={"exp": dev}, device_id_type=MESH)

    own = (
        pltpu.make_async_copy(tok_ref, xb.at[z, e], lsem.at[0]),
        pltpu.make_async_copy(dy_ref, db.at[z, e], lsem.at[1]),
        pltpu.make_async_copy(gate_ref, gb.at[e], lsem.at[2]),
    )
    for c in own:
        c.start()
    for c in weights(z, 1):
        c.start()

    @pl.when(z > 0)
    def _():
        for c in weights(z - 1, 0):
            c.start()

    barrier = pltpu.get_barrier_semaphore()
    pl.semaphore_signal(barrier, inc=1, device_id={"exp": mate}, device_id_type=MESH)
    pl.semaphore_signal(barrier, inc=1, device_id={"exp": across}, device_id_type=MESH)

    @pl.when(z > 0)
    def _():
        pl.semaphore_signal(barrier, inc=1, device_id={"hid": z - 1}, device_id_type=MESH)

    @pl.when(z < nz - 1)
    def _():
        pl.semaphore_signal(barrier, inc=1, device_id={"hid": z + 1}, device_id_type=MESH)

    peers = 2 + (z > 0).astype(jnp.int32) + (z < nz - 1).astype(jnp.int32)
    pl.semaphore_wait(barrier, peers)

    for c in own:
        c.wait()
    for a in range(2):
        @pl.when(z < nz - 1)
        def _():
            up(a, z).start()

        @pl.when(z > 0)
        def _():
            down(a, z).start()

        over_x(a, z).start()
        to_mate(a, z, e, 0).start()
    gate_send(e, 0, across).start()
    gate_send(e, 1, mate).start()

    pg[...] = jnp.zeros_like(pg)
    pu[...] = jnp.zeros_like(pu)
    dh[...] = jnp.zeros_like(dh)

    def pass_on(d):
        for a in range(2):
            @pl.when(z - d >= 0)
            def _():
                arrived(a, z - d, e)

                @pl.when(z < nz - 1)
                def _():
                    up(a, z - d).start()

                over_x(a, z - d).start()
                to_mate(a, z - d, e, 0).start()

            @pl.when(z + d < nz)
            def _():
                arrived(a, z + d, e)

                @pl.when(z > 0)
                def _():
                    down(a, z + d).start()

                over_x(a, z + d).start()
                to_mate(a, z + d, e, 0).start()

    def from_x(zq):
        for a in range(2):
            arrived(a, zq, across)
            to_mate(a, zq, across, 1).start()

    def compute(zq, slot):
        mate_across = lax.rem(mate + 2, ne)
        for a in range(2):
            arrived(a, zq, mate)
            arrived(a, zq, mate_across)
        for c in weights(zq, slot):
            c.wait()
        pick = pick_ref[...]
        xs = jnp.dot(pick, xb[zq].reshape(ne * tok, width), preferred_element_type=jnp.float32).astype(jnp.bfloat16)
        ds = jnp.dot(pick, db[zq].reshape(ne * tok, width), preferred_element_type=jnp.float32).astype(jnp.bfloat16)

        @pl.loop(0, hidden // TILE)
        def _(t):
            cols = pl.ds(pl.multiple_of(t * TILE, TILE), TILE)
            pg[:, cols] += jnp.dot(xs, w1[slot, :, cols], preferred_element_type=jnp.float32)
            pu[:, cols] += jnp.dot(xs, w3[slot, :, cols], preferred_element_type=jnp.float32)
            dh[:, cols] += lax.dot_general(ds, w2[slot, cols, :], CONTRACT_LAST, preferred_element_type=jnp.float32)

    @pl.loop(0, nz)
    def _(d):
        @pl.when((d > 0) & (z - d >= 0))
        def _():
            from_x(z - d)

        @pl.when(z + d < nz)
        def _():
            from_x(z + d)

        @pl.when(d < nz - 1)
        def _():
            pass_on(d + 1)

        @pl.when((d > 0) & (z - d >= 0))
        def _():
            compute(z - d, 0)

            @pl.when(z - d - 1 >= 0)
            def _():
                for c in weights(z - d - 1, 0):
                    c.start()

        @pl.when(z + d < nz)
        def _():
            compute(z + d, 1)

            @pl.when(z + d + 1 < nz)
            def _():
                for c in weights(z + d + 1, 1):
                    c.start()

    gate_send(across, 2, across).wait_recv()
    gate_send(across, 2, mate).start()
    gate_send(mate, 2, mate).wait_recv()
    gate_send(lax.rem(mate + 2, ne), 2, mate).wait_recv()
    gates = jnp.dot(pick_ref[...], gb[...].reshape(ne * tok, gb.shape[2]), preferred_element_type=jnp.float32)
    gate = jnp.sum(gates * slot_ref[...], axis=1, keepdims=True)
    score_ref[...] = jnp.zeros_like(score_ref)

    @pl.loop(0, hidden // 128)
    def _(t):
        cols = pl.ds(pl.multiple_of(t * 128, 128), 128)
        g = pg[:, cols]
        u = pu[:, cols]
        h = dh[:, cols]
        sig = 1.0 / (1.0 + jnp.exp(-g))
        act = g * sig
        score_ref[...] += act * u * h
        scaled = gate * h
        dpg_ref[:, cols] = (scaled * u * sig * (1.0 + g * (1.0 - sig))).astype(jnp.bfloat16)
        dpu_ref[:, cols] = (scaled * act).astype(jnp.bfloat16)

    @pl.loop(0, nz)
    def _(q):
        for a in range(2):
            @pl.when((q <= z) & (z < nz - 1))
            def _():
                up(a, q).wait_send()

            @pl.when((q >= z) & (z > 0))
            def _():
                down(a, q).wait_send()

            over_x(a, q).wait_send()
            to_mate(a, q, e, 0).wait_send()
            to_mate(a, q, across, 1).wait_send()
    gate_send(e, 0, across).wait_send()
    gate_send(e, 1, mate).wait_send()
    gate_send(across, 2, mate).wait_send()


def dispatched(tokens, grad_out, gates, pick, slots, w_gate, w_up, w_down):
    nz, ne = lax.axis_size("hid"), lax.axis_size("exp")
    tok, width = tokens.shape
    hidden = w_gate.shape[2]
    used = pick.shape[0]
    hbm = pl.BlockSpec(memory_space=pl.ANY)
    vmem = pl.BlockSpec(memory_space=pltpu.VMEM)
    bf16, f32 = jnp.bfloat16, jnp.float32
    dma = pltpu.SemaphoreType.DMA
    return pl.pallas_call(
        functools.partial(dispatch_kernel, nz, ne, tok, width),
        out_shape=(
            jax.ShapeDtypeStruct((used, hidden), bf16),
            jax.ShapeDtypeStruct((used, hidden), bf16),
            jax.ShapeDtypeStruct((used, 128), f32),
        ),
        in_specs=[hbm, hbm, hbm, vmem, vmem, hbm, hbm, hbm],
        out_specs=(vmem, vmem, vmem),
        scratch_shapes=[
            pltpu.VMEM((nz, ne, tok, width), bf16),
            pltpu.VMEM((nz, ne, tok, width), bf16),
            pltpu.VMEM((ne, tok, 128), bf16),
            pltpu.VMEM((2, width, hidden), bf16),
            pltpu.VMEM((2, width, hidden), bf16),
            pltpu.VMEM((2, hidden, width), bf16),
            pltpu.VMEM((used, hidden), f32),
            pltpu.VMEM((used, hidden), f32),
            pltpu.VMEM((used, hidden), f32),
            dma((2, nz)),
            dma((2, nz)),
            dma((2, nz)),
            dma((2, nz, 2)),
            dma((2, nz, ne)),
            dma((3,)),
            dma((ne,)),
            dma((2, 3)),
            dma((3,)),
        ],
        compiler_params=pltpu.CompilerParams(
            collective_id=0, has_side_effects=True, vmem_limit_bytes=56 * 1024 * 1024
        ),
        cost_estimate=pl.CostEstimate(
            flops=6 * used * hidden * width * nz,
            bytes_accessed=6 * hidden * width * nz,
            transcendentals=used * hidden,
        ),
        name="dispatch",
    )(tokens, grad_out, gates, pick, slots, w_gate, w_up, w_down)


def fast_local(tokens, grad_out, gates, block_experts, w_gate, w_up, w_down):
    n_experts = lax.axis_size("exp")
    own_index = lax.axis_index("exp")
    tok_dev, width_dev = tokens.shape
    blocks_all = block_experts.shape[0]
    per_home = tok_dev // BLOCK
    capacity = blocks_all // 2
    used_count = capacity * BLOCK
    list_block, list_slot, live = routing(block_experts, own_index)
    slot_hot = (list_slot[:, None] == jnp.arange(2, dtype=jnp.int32)[None, :]).astype(jnp.float32)
    slot_hot = slot_hot * live[:, None].astype(jnp.float32)
    row = jnp.where(live, list_block * BLOCK, -used_count * n_experts)[:, None] + jnp.arange(BLOCK, dtype=jnp.int32)[None, :]
    row = row.reshape(used_count, 1)
    pick = (row == jnp.arange(blocks_all * BLOCK, dtype=jnp.int32)[None, :]).astype(jnp.bfloat16)
    lane = jnp.arange(128, dtype=jnp.int32)[None, None, :]
    slots = ((list_slot[:, None, None] == lane) & live[:, None, None]).astype(jnp.float32)
    slots = jnp.broadcast_to(slots, (capacity, BLOCK, 128)).reshape(used_count, 128)
    gates_wide = jnp.pad(gates, ((0, 0), (0, 126)))
    d_pre_gate, d_pre_up, score_lanes = dispatched(
        tokens, grad_out, gates_wide, pick, slots, w_gate, w_up, w_down
    )
    score = lax.psum(jnp.sum(score_lanes, axis=1), "hid")
    first = lax.dot_general(w_gate[0], d_pre_gate, CONTRACT_LAST, preferred_element_type=jnp.float32)
    owned = lax.psum_scatter(
        first
        + lax.dot_general(w_up[0], d_pre_up, CONTRACT_LAST, preferred_element_type=jnp.float32),
        "hid",
        scatter_dimension=0,
        tiled=True,
    )
    return combined(owned, score, list_block, live, slot_hot, tok_dev, width_dev, capacity)


def combined(owned, score, list_block, live, slot_hot, tok_dev, width_dev, capacity):
    n_experts = lax.axis_size("exp")
    own_index = lax.axis_index("exp")
    per_home = tok_dev // BLOCK
    result_cols = owned.reshape(width_dev, capacity, BLOCK)
    score_blocks = score.reshape(capacity, BLOCK)

    def share(home):
        wanted = home * per_home + jnp.arange(per_home, dtype=jnp.int32)
        select = ((list_block[None, :] == wanted[:, None]) & live[None, :]).astype(jnp.float32)
        grad_part = jnp.einsum("bi,dir->dbr", select, result_cols, precision=HIGHEST).reshape(
            width_dev, tok_dev
        )
        gate_part = jnp.einsum(
            "bi,ik,ir->kbr", select, slot_hot, score_blocks, precision=HIGHEST
        ).reshape(2, tok_dev)
        return (grad_part, gate_part)

    zero_totals = (
        jnp.zeros((width_dev, tok_dev), jnp.float32),
        jnp.zeros((2, tok_dev), jnp.float32),
    )

    def single_turn(step, totals):
        grad_part, gate_part = share((own_index + 1 + step) % n_experts)
        return passed_along((totals[0] + grad_part, totals[1] + gate_part), "exp", -1)

    totals = lax.fori_loop(0, n_experts - 1, single_turn, zero_totals)
    grad_part, gate_part = share(own_index)
    grad_total = totals[0] + grad_part
    gate_total = totals[1] + gate_part
    return (grad_total.T.astype(jnp.bfloat16), gate_total.T)


def local(tokens, grad_out, gates, block_experts, w_gate, w_up, w_down):
    own_index = lax.axis_index("exp")
    tok_dev, width_dev = tokens.shape
    blocks_all = block_experts.shape[0]
    capacity = blocks_all // 2
    used_count = capacity * BLOCK
    list_block, list_slot, live = routing(block_experts, own_index)
    row_index = (list_block[:, None] * BLOCK + jnp.arange(BLOCK, dtype=jnp.int32)[None, :]).reshape(
        used_count
    )
    x_home, dy_home, gate_home = (
        lax.all_gather(tokens, "exp", axis=0, tiled=True),
        lax.all_gather(grad_out, "exp", axis=0, tiled=True),
        lax.all_gather(gates, "exp", axis=0, tiled=True),
    )
    gate_pick = (
        jnp.take(gate_home, row_index, axis=0).astype(jnp.float32).reshape(capacity, BLOCK, 2)
    )
    slot_hot = (list_slot[:, None] == jnp.arange(2, dtype=jnp.int32)[None, :]).astype(jnp.float32)
    slot_hot = slot_hot * live[:, None].astype(jnp.float32)
    gate_column = jnp.sum(gate_pick * slot_hot[:, None, :], axis=2).reshape(used_count)
    x_piece = jnp.take(lax.all_gather(x_home, "hid", axis=1, tiled=True), row_index, axis=0)
    dy_piece = jnp.take(lax.all_gather(dy_home, "hid", axis=1, tiled=True), row_index, axis=0)
    pre_gate = jnp.dot(x_piece, w_gate[0], preferred_element_type=jnp.float32)
    pre_up = jnp.dot(x_piece, w_up[0], preferred_element_type=jnp.float32)
    d_hidden = lax.dot_general(dy_piece, w_down[0], CONTRACT_LAST, preferred_element_type=jnp.float32)
    sigmoid_gate = jax.nn.sigmoid(pre_gate)
    activated = pre_gate * sigmoid_gate
    score_part = jnp.sum(activated * pre_up * d_hidden, axis=1)
    score = lax.psum(score_part, "hid")
    scaled = gate_column[:, None] * d_hidden
    d_pre_gate = (scaled * pre_up * sigmoid_gate * (1.0 + pre_gate * (1.0 - sigmoid_gate))).astype(
        jnp.bfloat16
    )
    d_pre_up = (scaled * activated).astype(jnp.bfloat16)
    first = lax.dot_general(w_gate[0], d_pre_gate, CONTRACT_LAST, preferred_element_type=jnp.float32)
    owned = lax.psum_scatter(
        first
        + lax.dot_general(w_up[0], d_pre_up, CONTRACT_LAST, preferred_element_type=jnp.float32),
        "hid",
        scatter_dimension=0,
        tiled=True,
    )
    return combined(owned, score, list_block, live, slot_hot, tok_dev, width_dev, capacity)


def solution(mesh):
    placed = (
        P(("grp", "exp"), "hid"),
        P(("grp", "exp"), "hid"),
        P(("grp", "exp"), None),
        P("grp", None),
        P("exp", None, "hid"),
        P("exp", None, "hid"),
        P("exp", "hid", None),
    )
    body = fast_local if mesh.shape["exp"] == 4 else local
    return jax.shard_map(
        body,
        mesh=mesh,
        in_specs=placed,
        out_specs=(P(("grp", "exp"), "hid"), P(("grp", "exp"), None)),
        check_vma=False,
    )
```

```python
import functools
import jax
import jax.numpy as jnp
from jax import lax
from jax.experimental import pallas as pl
from jax.experimental.pallas import tpu as pltpu
from jax.sharding import PartitionSpec as P

BLOCK = 128


HIGHEST = lax.Precision.HIGHEST
CONTRACT_LAST = (((1,), (1,)), ((), ()))
MESH = pl.DeviceIdType.MESH
TILE = 512


def passed_along(block, axis, distance):
    devices = range(lax.axis_size(axis))
    route = [((i - distance) % len(devices), i) for i in devices]
    return lax.ppermute(block, axis, route)


def routing(block_experts, own_index):
    blocks_all = block_experts.shape[0]
    capacity = blocks_all // 2
    matched = block_experts == own_index
    chosen = jnp.any(matched, axis=1)
    slot_of = matched[:, 1].astype(jnp.int32)
    position = jnp.cumsum(chosen.astype(jnp.int32)) - 1
    placed = (position[None, :] == jnp.arange(capacity, dtype=jnp.int32)[:, None]) & chosen[None, :]
    placed_int = placed.astype(jnp.int32)
    list_block = jnp.sum(placed_int * jnp.arange(blocks_all, dtype=jnp.int32)[None, :], axis=1)
    list_slot = jnp.sum(placed_int * slot_of[None, :], axis=1)
    live = jnp.any(placed, axis=1)
    return list_block, list_slot, live


def dispatch_kernel(nz, ne, tok, width, tok_ref, dy_ref, gate_ref, pick_ref, slot_ref, w1_ref, w3_ref, w2_ref,
                    dpg_ref, dpu_ref, score_ref,
                    xb, db, gb, w1, w3, w2, pg, pu, dh,
                    s_up, s_dn, s_x, s_c, rsem, gs, gr, wsem, lsem):
    z = lax.axis_index("hid")
    e = lax.axis_index("exp")
    mate = e + 1 - 2 * lax.rem(e, 2)
    across = lax.rem(e + 2, ne)
    bufs = (xb, db)
    hidden = w1.shape[2]

    def weights(q, slot):
        rows = pl.ds(pl.multiple_of(q * width, width), width)
        return (
            pltpu.make_async_copy(w1_ref.at[0, rows, :], w1.at[slot], wsem.at[slot, 0]),
            pltpu.make_async_copy(w3_ref.at[0, rows, :], w3.at[slot], wsem.at[slot, 1]),
            pltpu.make_async_copy(w2_ref.at[0, :, rows], w2.at[slot], wsem.at[slot, 2]),
        )

    def send(a, zq, eq, ssem, dev):
        return pltpu.make_async_remote_copy(
            src_ref=bufs[a].at[zq, eq], dst_ref=bufs[a].at[zq, eq],
            send_sem=ssem, recv_sem=rsem.at[a, zq, eq],
            device_id=dev, device_id_type=MESH)

    def up(a, zq):
        return send(a, zq, e, s_up.at[a, zq], {"hid": z + 1})

    def down(a, zq):
        return send(a, zq, e, s_dn.at[a, zq], {"hid": z - 1})

    def over_x(a, zq):
        return send(a, zq, e, s_x.at[a, zq], {"exp": across})

    def to_mate(a, zq, eq, k):
        return send(a, zq, eq, s_c.at[a, zq, k], {"exp": mate})

    def arrived(a, zq, eq):
        send(a, zq, eq, s_x.at[a, zq], {"exp": across}).wait_recv()

    def gate_send(eq, k, dev):
        return pltpu.make_async_remote_copy(
            src_ref=gb.at[eq], dst_ref=gb.at[eq], send_sem=gs.at[k], recv_sem=gr.at[eq],
            device_id={"exp": dev}, device_id_type=MESH)

    own = (
        pltpu.make_async_copy(tok_ref, xb.at[z, e], lsem.at[0]),
        pltpu.make_async_copy(dy_ref, db.at[z, e], lsem.at[1]),
        pltpu.make_async_copy(gate_ref, gb.at[e], lsem.at[2]),
    )
    for c in own:
        c.start()
    for c in weights(z, 1):
        c.start()

    @pl.when(z > 0)
    def _():
        for c in weights(z - 1, 0):
            c.start()

    barrier = pltpu.get_barrier_semaphore()
    pl.semaphore_signal(barrier, inc=1, device_id={"exp": mate}, device_id_type=MESH)
    pl.semaphore_signal(barrier, inc=1, device_id={"exp": across}, device_id_type=MESH)

    @pl.when(z > 0)
    def _():
        pl.semaphore_signal(barrier, inc=1, device_id={"hid": z - 1}, device_id_type=MESH)

    @pl.when(z < nz - 1)
    def _():
        pl.semaphore_signal(barrier, inc=1, device_id={"hid": z + 1}, device_id_type=MESH)

    peers = 2 + (z > 0).astype(jnp.int32) + (z < nz - 1).astype(jnp.int32)
    pl.semaphore_wait(barrier, peers)

    for c in own:
        c.wait()
    for a in range(2):
        @pl.when(z < nz - 1)
        def _():
            up(a, z).start()

        @pl.when(z > 0)
        def _():
            down(a, z).start()

        over_x(a, z).start()
        to_mate(a, z, e, 0).start()
    gate_send(e, 0, across).start()
    gate_send(e, 1, mate).start()

    pg[...] = jnp.zeros_like(pg)
    pu[...] = jnp.zeros_like(pu)
    dh[...] = jnp.zeros_like(dh)

    def pass_on(d):
        for a in range(2):
            @pl.when(z - d >= 0)
            def _():
                arrived(a, z - d, e)

                @pl.when(z < nz - 1)
                def _():
                    up(a, z - d).start()

                over_x(a, z - d).start()
                to_mate(a, z - d, e, 0).start()

            @pl.when(z + d < nz)
            def _():
                arrived(a, z + d, e)

                @pl.when(z > 0)
                def _():
                    down(a, z + d).start()

                over_x(a, z + d).start()
                to_mate(a, z + d, e, 0).start()

    def from_x(zq):
        for a in range(2):
            arrived(a, zq, across)
            to_mate(a, zq, across, 1).start()

    def compute(zq, slot):
        mate_across = lax.rem(mate + 2, ne)
        for a in range(2):
            arrived(a, zq, mate)
            arrived(a, zq, mate_across)
        for c in weights(zq, slot):
            c.wait()
        pick = pick_ref[...]
        xs = jnp.dot(pick, xb[zq].reshape(ne * tok, width), preferred_element_type=jnp.float32).astype(jnp.bfloat16)
        ds = jnp.dot(pick, db[zq].reshape(ne * tok, width), preferred_element_type=jnp.float32).astype(jnp.bfloat16)

        @pl.loop(0, hidden // TILE)
        def _(t):
            cols = pl.ds(pl.multiple_of(t * TILE, TILE), TILE)
            pg[:, cols] += jnp.dot(xs, w1[slot, :, cols], preferred_element_type=jnp.float32)
            pu[:, cols] += jnp.dot(xs, w3[slot, :, cols], preferred_element_type=jnp.float32)
            dh[:, cols] += lax.dot_general(ds, w2[slot, cols, :], CONTRACT_LAST, preferred_element_type=jnp.float32)

    @pl.loop(0, nz)
    def _(d):
        @pl.when((d > 0) & (z - d >= 0))
        def _():
            from_x(z - d)

        @pl.when(z + d < nz)
        def _():
            from_x(z + d)

        @pl.when(d < nz - 1)
        def _():
            pass_on(d + 1)

        @pl.when((d > 0) & (z - d >= 0))
        def _():
            compute(z - d, 0)

            @pl.when(z - d - 1 >= 0)
            def _():
                for c in weights(z - d - 1, 0):
                    c.start()

        @pl.when(z + d < nz)
        def _():
            compute(z + d, 1)

            @pl.when(z + d + 1 < nz)
            def _():
                for c in weights(z + d + 1, 1):
                    c.start()

    gate_send(across, 2, across).wait_recv()
    gate_send(across, 2, mate).start()
    gate_send(mate, 2, mate).wait_recv()
    gate_send(lax.rem(mate + 2, ne), 2, mate).wait_recv()
    gates = jnp.dot(pick_ref[...], gb[...].reshape(ne * tok, gb.shape[2]), preferred_element_type=jnp.float32)
    gate = jnp.sum(gates * slot_ref[...], axis=1, keepdims=True)
    score_ref[...] = jnp.zeros_like(score_ref)

    @pl.loop(0, hidden // 128)
    def _(t):
        cols = pl.ds(pl.multiple_of(t * 128, 128), 128)
        g = pg[:, cols]
        u = pu[:, cols]
        h = dh[:, cols]
        sig = 1.0 / (1.0 + jnp.exp(-g))
        act = g * sig
        score_ref[...] += act * u * h
        scaled = gate * h
        dpg_ref[:, cols] = (scaled * u * sig * (1.0 + g * (1.0 - sig))).astype(jnp.bfloat16)
        dpu_ref[:, cols] = (scaled * act).astype(jnp.bfloat16)

    @pl.loop(0, nz)
    def _(q):
        for a in range(2):
            @pl.when((q <= z) & (z < nz - 1))
            def _():
                up(a, q).wait_send()

            @pl.when((q >= z) & (z > 0))
            def _():
                down(a, q).wait_send()

            over_x(a, q).wait_send()
            to_mate(a, q, e, 0).wait_send()
            to_mate(a, q, across, 1).wait_send()
    gate_send(e, 0, across).wait_send()
    gate_send(e, 1, mate).wait_send()
    gate_send(across, 2, mate).wait_send()


def dispatched(tokens, grad_out, gates, pick, slots, w_gate, w_up, w_down):
    nz, ne = lax.axis_size("hid"), lax.axis_size("exp")
    tok, width = tokens.shape
    hidden = w_gate.shape[2]
    used = pick.shape[0]
    hbm = pl.BlockSpec(memory_space=pl.ANY)
    vmem = pl.BlockSpec(memory_space=pltpu.VMEM)
    bf16, f32 = jnp.bfloat16, jnp.float32
    dma = pltpu.SemaphoreType.DMA
    return pl.pallas_call(
        functools.partial(dispatch_kernel, nz, ne, tok, width),
        out_shape=(
            jax.ShapeDtypeStruct((used, hidden), bf16),
            jax.ShapeDtypeStruct((used, hidden), bf16),
            jax.ShapeDtypeStruct((used, 128), f32),
        ),
        in_specs=[hbm, hbm, hbm, vmem, vmem, hbm, hbm, hbm],
        out_specs=(vmem, vmem, vmem),
        scratch_shapes=[
            pltpu.VMEM((nz, ne, tok, width), bf16),
            pltpu.VMEM((nz, ne, tok, width), bf16),
            pltpu.VMEM((ne, tok, 128), bf16),
            pltpu.VMEM((2, width, hidden), bf16),
            pltpu.VMEM((2, width, hidden), bf16),
            pltpu.VMEM((2, hidden, width), bf16),
            pltpu.VMEM((used, hidden), f32),
            pltpu.VMEM((used, hidden), f32),
            pltpu.VMEM((used, hidden), f32),
            dma((2, nz)),
            dma((2, nz)),
            dma((2, nz)),
            dma((2, nz, 2)),
            dma((2, nz, ne)),
            dma((3,)),
            dma((ne,)),
            dma((2, 3)),
            dma((3,)),
        ],
        compiler_params=pltpu.CompilerParams(
            collective_id=0, has_side_effects=True, vmem_limit_bytes=56 * 1024 * 1024
        ),
        cost_estimate=pl.CostEstimate(
            flops=6 * used * hidden * width * nz,
            bytes_accessed=6 * hidden * width * nz,
            transcendentals=used * hidden,
        ),
        name="dispatch",
    )(tokens, grad_out, gates, pick, slots, w_gate, w_up, w_down)


def combine_kernel(nz, ne, tok, width, dpg_ref, dpu_ref, scat_ref, sd_ref, w1_ref, w3_ref, out_ref, gate_ref,
                   dense, cr, xs, xr, zs, zr, acc, w1, w3, scr, sxs, sxr, szs, szr,
                   css, crs, xss, xrs, zss, zrs, gcs, gcr, gxs, gxr, gzs, gzr, wsem):
    z = lax.axis_index("hid")
    e = lax.axis_index("exp")
    core = lax.rem(e, 2)
    mate = e + 1 - 2 * core
    mate_core = 1 - core
    across = lax.rem(e + 2, ne)
    x = e // 2
    far = 1 - x

    def weights(k, slot):
        q = lax.rem(z + 1 + k, nz)
        rows = pl.ds(pl.multiple_of(q * width, width), width)
        return (
            pltpu.make_async_copy(w1_ref.at[0, rows, :], w1.at[slot], wsem.at[slot, 0]),
            pltpu.make_async_copy(w3_ref.at[0, rows, :], w3.at[slot], wsem.at[slot, 1]),
        )

    def remote(src, dst, ssem, rsem, dev):
        return pltpu.make_async_remote_copy(
            src_ref=src, dst_ref=dst, send_sem=ssem, recv_sem=rsem, device_id=dev, device_id_type=MESH)

    def core_send(k, j):
        return remote(dense.at[k, mate_core + 2 * j], cr.at[k, j], css.at[k, j], crs.at[k, j], {"exp": mate})

    def x_send(k):
        return remote(xs.at[k], xr.at[k], xss.at[k], xrs.at[k], {"exp": across})

    def z_send(k):
        return remote(zs.at[k], zr.at[z], zss.at[k], zrs.at[z], {"hid": lax.rem(z + 1 + k, nz)})

    def gate_core(j):
        return remote(sd_ref.at[mate_core + 2 * j], scr.at[j], gcs.at[j], gcr.at[j], {"exp": mate})

    def gate_x():
        return remote(sxs, sxr, gxs.at[0], gxr.at[0], {"exp": across})

    def gate_z(k):
        return remote(szs, szr.at[z], gzs.at[k], gzr.at[z], {"hid": lax.rem(z + 1 + k, nz)})

    for k in range(2):
        for c in weights(k, k):
            c.start()

    barrier = pltpu.get_barrier_semaphore()
    pl.semaphore_signal(barrier, inc=1, device_id={"exp": mate}, device_id_type=MESH)
    pl.semaphore_signal(barrier, inc=1, device_id={"exp": across}, device_id_type=MESH)
    for k in range(nz - 1):
        pl.semaphore_signal(barrier, inc=1, device_id={"hid": lax.rem(z + 1 + k, nz)}, device_id_type=MESH)
    pl.semaphore_wait(barrier, nz + 1)

    for j in range(2):
        gate_core(j).start()

    def multiply(k):
        slot = lax.rem(k, 2)
        for c in weights(k, slot):
            c.wait()

        @pl.loop(0, width // 256)
        def _(t):
            rows = pl.ds(pl.multiple_of(t * 256, 256), 256)
            part = lax.dot_general(dpg_ref[...], w1[slot, rows, :], CONTRACT_LAST, preferred_element_type=jnp.float32)
            part += lax.dot_general(dpu_ref[...], w3[slot, rows, :], CONTRACT_LAST, preferred_element_type=jnp.float32)
            spread = jnp.dot(scat_ref[...], part.astype(jnp.bfloat16), preferred_element_type=jnp.float32)
            dense[k, :, :, rows] = spread.astype(jnp.bfloat16).reshape(ne, tok, 256)

        for j in range(2):
            core_send(k, j).start()

        @pl.when(k + 2 < nz)
        def _():
            for c in weights(k + 2, slot):
                c.start()

    def to_x(k):
        for j in range(2):
            core_send(k, j).wait_recv()
        both = dense[k, core + 2 * far].astype(jnp.float32) + cr[k, far].astype(jnp.float32)
        xs[k] = both.astype(jnp.bfloat16)
        x_send(k).start()

    def total(k):
        x_send(k).wait_recv()
        return (
            dense[k, e].astype(jnp.float32) + cr[k, x].astype(jnp.float32) + xr[k].astype(jnp.float32)
        )

    def to_z(k):
        zs[k] = total(k).astype(jnp.bfloat16)
        z_send(k).start()

    @pl.loop(0, nz)
    def _(k):
        multiply(k)
        to_x(k)

        @pl.when(k == 0)
        def _():
            for j in range(2):
                gate_core(j).wait_recv()
            sxs[...] = sd_ref[core + 2 * far] + scr[far]
            gate_x().start()

        @pl.when(k == 1)
        def _():
            gate_x().wait_recv()
            own_sum = sd_ref[e] + scr[x] + sxr[...]
            szs[...] = own_sum
            szr[z] = own_sum
            for i in range(nz - 1):
                gate_z(i).start()

        @pl.when(k >= 2)
        def _():
            to_z(k - 2)

    to_z(nz - 2)
    acc[...] = total(nz - 1)
    for k in range(nz - 1):
        source = lax.rem(z + 1 + k, nz)
        remote(zs.at[k], zr.at[source], zss.at[k], zrs.at[source], {"hid": source}).wait_recv()
        acc[...] += zr[source].astype(jnp.float32)
        remote(szs, szr.at[source], gzs.at[k], gzr.at[source], {"hid": source}).wait_recv()
    out_ref[...] = acc[...].astype(jnp.bfloat16)
    gate_total = szr[0]
    for q in range(1, nz):
        gate_total += szr[q]
    gate_ref[...] = gate_total

    for j in range(2):
        gate_core(j).wait_send()
    gate_x().wait_send()
    for k in range(nz):
        for j in range(2):
            core_send(k, j).wait_send()
        x_send(k).wait_send()
        if k < nz - 1:
            z_send(k).wait_send()
            gate_z(k).wait_send()


def returned(d_pre_gate, d_pre_up, scatter, score_dense, w_gate, w_up, tok, width):
    nz, ne = lax.axis_size("hid"), lax.axis_size("exp")
    used, hidden = d_pre_gate.shape
    hbm = pl.BlockSpec(memory_space=pl.ANY)
    vmem = pl.BlockSpec(memory_space=pltpu.VMEM)
    bf16, f32 = jnp.bfloat16, jnp.float32
    dma = pltpu.SemaphoreType.DMA
    return pl.pallas_call(
        functools.partial(combine_kernel, nz, ne, tok, width),
        out_shape=(
            jax.ShapeDtypeStruct((tok, width), bf16),
            jax.ShapeDtypeStruct((8, tok), f32),
        ),
        in_specs=[vmem, vmem, vmem, vmem, hbm, hbm],
        out_specs=(vmem, vmem),
        scratch_shapes=[
            pltpu.VMEM((nz, ne, tok, width), bf16),
            pltpu.VMEM((nz, 2, tok, width), bf16),
            pltpu.VMEM((nz, tok, width), bf16),
            pltpu.VMEM((nz, tok, width), bf16),
            pltpu.VMEM((nz, tok, width), bf16),
            pltpu.VMEM((nz, tok, width), bf16),
            pltpu.VMEM((tok, width), f32),
            pltpu.VMEM((2, width, hidden), bf16),
            pltpu.VMEM((2, width, hidden), bf16),
            pltpu.VMEM((2, 8, tok), f32),
            pltpu.VMEM((8, tok), f32),
            pltpu.VMEM((8, tok), f32),
            pltpu.VMEM((8, tok), f32),
            pltpu.VMEM((nz, 8, tok), f32),
            dma((nz, 2)),
            dma((nz, 2)),
            dma((nz,)),
            dma((nz,)),
            dma((nz,)),
            dma((nz,)),
            dma((2,)),
            dma((2,)),
            dma((1,)),
            dma((1,)),
            dma((nz,)),
            dma((nz,)),
            dma((2, 2)),
        ],
        compiler_params=pltpu.CompilerParams(
            collective_id=1, has_side_effects=True, vmem_limit_bytes=52 * 1024 * 1024
        ),
        cost_estimate=pl.CostEstimate(
            flops=4 * used * hidden * width * nz,
            bytes_accessed=4 * hidden * width * nz,
            transcendentals=0,
        ),
        name="combine",
    )(d_pre_gate, d_pre_up, scatter, score_dense, w_gate, w_up)


def fast_local(tokens, grad_out, gates, block_experts, w_gate, w_up, w_down):
    n_experts = lax.axis_size("exp")
    own_index = lax.axis_index("exp")
    tok_dev, width_dev = tokens.shape
    blocks_all = block_experts.shape[0]
    per_home = tok_dev // BLOCK
    capacity = blocks_all // 2
    used_count = capacity * BLOCK
    list_block, list_slot, live = routing(block_experts, own_index)
    slot_hot = (list_slot[:, None] == jnp.arange(2, dtype=jnp.int32)[None, :]).astype(jnp.float32)
    slot_hot = slot_hot * live[:, None].astype(jnp.float32)
    row = jnp.where(live, list_block * BLOCK, -used_count * n_experts)[:, None] + jnp.arange(BLOCK, dtype=jnp.int32)[None, :]
    row = row.reshape(used_count, 1)
    pick = (row == jnp.arange(blocks_all * BLOCK, dtype=jnp.int32)[None, :]).astype(jnp.bfloat16)
    lane = jnp.arange(128, dtype=jnp.int32)[None, None, :]
    slots = ((list_slot[:, None, None] == lane) & live[:, None, None]).astype(jnp.float32)
    slots = jnp.broadcast_to(slots, (capacity, BLOCK, 128)).reshape(used_count, 128)
    gates_wide = jnp.pad(gates, ((0, 0), (0, 126)))
    d_pre_gate, d_pre_up, score_lanes = dispatched(
        tokens, grad_out, gates_wide, pick, slots, w_gate, w_up, w_down
    )
    score = jnp.sum(score_lanes, axis=1).reshape(capacity, BLOCK)
    homes = jnp.arange(blocks_all, dtype=jnp.int32)
    goes = (list_block[:, None] == homes[None, :]).astype(jnp.float32)[:, :, None] * slot_hot[:, None, :]
    goes = jnp.pad(goes, ((0, 0), (0, 0), (0, 6)))
    score_dense = jnp.sum(goes[:, :, :, None] * score[:, None, None, :], axis=0)
    grad, gate_rows = returned(
        d_pre_gate, d_pre_up, pick.T, score_dense, w_gate, w_up, tok_dev, width_dev
    )
    return grad, gate_rows[:2].T


def combined(owned, score, list_block, live, slot_hot, tok_dev, width_dev, capacity):
    n_experts = lax.axis_size("exp")
    own_index = lax.axis_index("exp")
    per_home = tok_dev // BLOCK
    result_cols = owned.reshape(width_dev, capacity, BLOCK)
    score_blocks = score.reshape(capacity, BLOCK)

    def share(home):
        wanted = home * per_home + jnp.arange(per_home, dtype=jnp.int32)
        select = ((list_block[None, :] == wanted[:, None]) & live[None, :]).astype(jnp.float32)
        grad_part = jnp.einsum("bi,dir->dbr", select, result_cols, precision=HIGHEST).reshape(
            width_dev, tok_dev
        )
        gate_part = jnp.einsum(
            "bi,ik,ir->kbr", select, slot_hot, score_blocks, precision=HIGHEST
        ).reshape(2, tok_dev)
        return (grad_part, gate_part)

    zero_totals = (
        jnp.zeros((width_dev, tok_dev), jnp.float32),
        jnp.zeros((2, tok_dev), jnp.float32),
    )

    def single_turn(step, totals):
        grad_part, gate_part = share((own_index + 1 + step) % n_experts)
        return passed_along((totals[0] + grad_part, totals[1] + gate_part), "exp", -1)

    totals = lax.fori_loop(0, n_experts - 1, single_turn, zero_totals)
    grad_part, gate_part = share(own_index)
    grad_total = totals[0] + grad_part
    gate_total = totals[1] + gate_part
    return (grad_total.T.astype(jnp.bfloat16), gate_total.T)


def local(tokens, grad_out, gates, block_experts, w_gate, w_up, w_down):
    own_index = lax.axis_index("exp")
    tok_dev, width_dev = tokens.shape
    blocks_all = block_experts.shape[0]
    capacity = blocks_all // 2
    used_count = capacity * BLOCK
    list_block, list_slot, live = routing(block_experts, own_index)
    row_index = (list_block[:, None] * BLOCK + jnp.arange(BLOCK, dtype=jnp.int32)[None, :]).reshape(
        used_count
    )
    x_home, dy_home, gate_home = (
        lax.all_gather(tokens, "exp", axis=0, tiled=True),
        lax.all_gather(grad_out, "exp", axis=0, tiled=True),
        lax.all_gather(gates, "exp", axis=0, tiled=True),
    )
    gate_pick = (
        jnp.take(gate_home, row_index, axis=0).astype(jnp.float32).reshape(capacity, BLOCK, 2)
    )
    slot_hot = (list_slot[:, None] == jnp.arange(2, dtype=jnp.int32)[None, :]).astype(jnp.float32)
    slot_hot = slot_hot * live[:, None].astype(jnp.float32)
    gate_column = jnp.sum(gate_pick * slot_hot[:, None, :], axis=2).reshape(used_count)
    x_piece = jnp.take(lax.all_gather(x_home, "hid", axis=1, tiled=True), row_index, axis=0)
    dy_piece = jnp.take(lax.all_gather(dy_home, "hid", axis=1, tiled=True), row_index, axis=0)
    pre_gate = jnp.dot(x_piece, w_gate[0], preferred_element_type=jnp.float32)
    pre_up = jnp.dot(x_piece, w_up[0], preferred_element_type=jnp.float32)
    d_hidden = lax.dot_general(dy_piece, w_down[0], CONTRACT_LAST, preferred_element_type=jnp.float32)
    sigmoid_gate = jax.nn.sigmoid(pre_gate)
    activated = pre_gate * sigmoid_gate
    score_part = jnp.sum(activated * pre_up * d_hidden, axis=1)
    score = lax.psum(score_part, "hid")
    scaled = gate_column[:, None] * d_hidden
    d_pre_gate = (scaled * pre_up * sigmoid_gate * (1.0 + pre_gate * (1.0 - sigmoid_gate))).astype(
        jnp.bfloat16
    )
    d_pre_up = (scaled * activated).astype(jnp.bfloat16)
    first = lax.dot_general(w_gate[0], d_pre_gate, CONTRACT_LAST, preferred_element_type=jnp.float32)
    owned = lax.psum_scatter(
        first
        + lax.dot_general(w_up[0], d_pre_up, CONTRACT_LAST, preferred_element_type=jnp.float32),
        "hid",
        scatter_dimension=0,
        tiled=True,
    )
    return combined(owned, score, list_block, live, slot_hot, tok_dev, width_dev, capacity)


def solution(mesh):
    placed = (
        P(("grp", "exp"), "hid"),
        P(("grp", "exp"), "hid"),
        P(("grp", "exp"), None),
        P("grp", None),
        P("exp", None, "hid"),
        P("exp", None, "hid"),
        P("exp", "hid", None),
    )
    body = fast_local if (mesh.shape["exp"], mesh.shape["hid"]) == (4, 4) else local
    return jax.shard_map(
        body,
        mesh=mesh,
        in_specs=placed,
        out_specs=(P(("grp", "exp"), "hid"), P(("grp", "exp"), None)),
        check_vma=False,
    )
```

```python
import functools
import jax
import jax.numpy as jnp
from jax import lax
from jax.experimental import pallas as pl
from jax.experimental.pallas import tpu as pltpu
from jax.sharding import PartitionSpec as P

BLOCK = 128


HIGHEST = lax.Precision.HIGHEST
CONTRACT_LAST = (((1,), (1,)), ((), ()))
MESH = pl.DeviceIdType.MESH
TILE = 512


def passed_along(block, axis, distance):
    devices = range(lax.axis_size(axis))
    route = [((i - distance) % len(devices), i) for i in devices]
    return lax.ppermute(block, axis, route)


def routing(block_experts, own_index):
    blocks_all = block_experts.shape[0]
    capacity = blocks_all // 2
    matched = block_experts == own_index
    chosen = jnp.any(matched, axis=1)
    slot_of = matched[:, 1].astype(jnp.int32)
    position = jnp.cumsum(chosen.astype(jnp.int32)) - 1
    placed = (position[None, :] == jnp.arange(capacity, dtype=jnp.int32)[:, None]) & chosen[None, :]
    placed_int = placed.astype(jnp.int32)
    list_block = jnp.sum(placed_int * jnp.arange(blocks_all, dtype=jnp.int32)[None, :], axis=1)
    list_slot = jnp.sum(placed_int * slot_of[None, :], axis=1)
    live = jnp.any(placed, axis=1)
    return list_block, list_slot, live


def dispatch_kernel(nz, ne, tok, width, tok_ref, dy_ref, gate_ref, pick_ref, slot_ref, w1_ref, w3_ref, w2_ref,
                    dpg_ref, dpu_ref, score_ref,
                    xb, db, gb, w1, w3, w2, pg, pu, dh,
                    s_up, s_dn, s_x, s_c, rsem, gs, gr, wsem, lsem):
    z = lax.axis_index("hid")
    e = lax.axis_index("exp")
    mate = e + 1 - 2 * lax.rem(e, 2)
    across = lax.rem(e + 2, ne)
    bufs = (xb, db)
    hidden = w1.shape[2]

    def weights(q, slot):
        rows = pl.ds(pl.multiple_of(q * width, width), width)
        return (
            pltpu.make_async_copy(w1_ref.at[0, rows, :], w1.at[slot], wsem.at[slot, 0]),
            pltpu.make_async_copy(w3_ref.at[0, rows, :], w3.at[slot], wsem.at[slot, 1]),
            pltpu.make_async_copy(w2_ref.at[0, :, rows], w2.at[slot], wsem.at[slot, 2]),
        )

    def send(a, zq, eq, ssem, dev):
        return pltpu.make_async_remote_copy(
            src_ref=bufs[a].at[zq, eq], dst_ref=bufs[a].at[zq, eq],
            send_sem=ssem, recv_sem=rsem.at[a, zq, eq],
            device_id=dev, device_id_type=MESH)

    def up(a, zq):
        return send(a, zq, e, s_up.at[a, zq], {"hid": z + 1})

    def down(a, zq):
        return send(a, zq, e, s_dn.at[a, zq], {"hid": z - 1})

    def over_x(a, zq):
        return send(a, zq, e, s_x.at[a, zq], {"exp": across})

    def to_mate(a, zq, eq, k):
        return send(a, zq, eq, s_c.at[a, zq, k], {"exp": mate})

    def arrived(a, zq, eq):
        send(a, zq, eq, s_x.at[a, zq], {"exp": across}).wait_recv()

    def gate_send(eq, k, dev):
        return pltpu.make_async_remote_copy(
            src_ref=gb.at[eq], dst_ref=gb.at[eq], send_sem=gs.at[k], recv_sem=gr.at[eq],
            device_id={"exp": dev}, device_id_type=MESH)

    own = (
        pltpu.make_async_copy(tok_ref, xb.at[z, e], lsem.at[0]),
        pltpu.make_async_copy(dy_ref, db.at[z, e], lsem.at[1]),
        pltpu.make_async_copy(gate_ref, gb.at[e], lsem.at[2]),
    )
    for c in own:
        c.start()
    for c in weights(z, 1):
        c.start()

    @pl.when(z > 0)
    def _():
        for c in weights(z - 1, 0):
            c.start()

    barrier = pltpu.get_barrier_semaphore()
    pl.semaphore_signal(barrier, inc=1, device_id={"exp": mate}, device_id_type=MESH)
    pl.semaphore_signal(barrier, inc=1, device_id={"exp": across}, device_id_type=MESH)

    @pl.when(z > 0)
    def _():
        pl.semaphore_signal(barrier, inc=1, device_id={"hid": z - 1}, device_id_type=MESH)

    @pl.when(z < nz - 1)
    def _():
        pl.semaphore_signal(barrier, inc=1, device_id={"hid": z + 1}, device_id_type=MESH)

    peers = 2 + (z > 0).astype(jnp.int32) + (z < nz - 1).astype(jnp.int32)
    pl.semaphore_wait(barrier, peers)

    for c in own:
        c.wait()
    for a in range(2):
        @pl.when(z < nz - 1)
        def _():
            up(a, z).start()

        @pl.when(z > 0)
        def _():
            down(a, z).start()

        over_x(a, z).start()
        to_mate(a, z, e, 0).start()
    gate_send(e, 0, across).start()
    gate_send(e, 1, mate).start()

    pg[...] = jnp.zeros_like(pg)
    pu[...] = jnp.zeros_like(pu)
    dh[...] = jnp.zeros_like(dh)

    def pass_on(d):
        for a in range(2):
            @pl.when(z - d >= 0)
            def _():
                arrived(a, z - d, e)

                @pl.when(z < nz - 1)
                def _():
                    up(a, z - d).start()

                over_x(a, z - d).start()
                to_mate(a, z - d, e, 0).start()

            @pl.when(z + d < nz)
            def _():
                arrived(a, z + d, e)

                @pl.when(z > 0)
                def _():
                    down(a, z + d).start()

                over_x(a, z + d).start()
                to_mate(a, z + d, e, 0).start()

    mate_across = lax.rem(mate + 2, ne)

    def picked(a, zq):
        arrived(a, zq, across)
        to_mate(a, zq, across, 1).start()
        arrived(a, zq, mate)
        arrived(a, zq, mate_across)
        rows = bufs[a][zq].reshape(ne * tok, width)
        return jnp.dot(pick_ref[...], rows, preferred_element_type=jnp.float32).astype(jnp.bfloat16)

    def compute(zq, slot):
        pending = weights(zq, slot)
        xs = picked(0, zq)
        pending[0].wait()
        pending[1].wait()

        @pl.loop(0, hidden // TILE)
        def _(t):
            cols = pl.ds(pl.multiple_of(t * TILE, TILE), TILE)
            pg[:, cols] += jnp.dot(xs, w1[slot, :, cols], preferred_element_type=jnp.float32)
            pu[:, cols] += jnp.dot(xs, w3[slot, :, cols], preferred_element_type=jnp.float32)

        ds = picked(1, zq)
        pending[2].wait()

        @pl.loop(0, hidden // TILE)
        def _(t):
            cols = pl.ds(pl.multiple_of(t * TILE, TILE), TILE)
            dh[:, cols] += lax.dot_general(ds, w2[slot, cols, :], CONTRACT_LAST, preferred_element_type=jnp.float32)

    @pl.loop(0, nz)
    def _(d):
        @pl.when(d < nz - 1)
        def _():
            pass_on(d + 1)

        @pl.when((d > 0) & (z - d >= 0))
        def _():
            compute(z - d, 0)

            @pl.when(z - d - 1 >= 0)
            def _():
                for c in weights(z - d - 1, 0):
                    c.start()

        @pl.when(z + d < nz)
        def _():
            compute(z + d, 1)

            @pl.when(z + d + 1 < nz)
            def _():
                for c in weights(z + d + 1, 1):
                    c.start()

    gate_send(across, 2, across).wait_recv()
    gate_send(across, 2, mate).start()
    gate_send(mate, 2, mate).wait_recv()
    gate_send(lax.rem(mate + 2, ne), 2, mate).wait_recv()
    gates = jnp.dot(pick_ref[...], gb[...].reshape(ne * tok, gb.shape[2]), preferred_element_type=jnp.float32)
    gate = jnp.sum(gates * slot_ref[...], axis=1, keepdims=True)
    score_ref[...] = jnp.zeros_like(score_ref)

    @pl.loop(0, hidden // 128)
    def _(t):
        cols = pl.ds(pl.multiple_of(t * 128, 128), 128)
        g = pg[:, cols]
        u = pu[:, cols]
        h = dh[:, cols]
        sig = 1.0 / (1.0 + jnp.exp(-g))
        act = g * sig
        score_ref[...] += act * u * h
        scaled = gate * h
        dpg_ref[:, cols] = (scaled * u * sig * (1.0 + g * (1.0 - sig))).astype(jnp.bfloat16)
        dpu_ref[:, cols] = (scaled * act).astype(jnp.bfloat16)

    @pl.loop(0, nz)
    def _(q):
        for a in range(2):
            @pl.when((q <= z) & (z < nz - 1))
            def _():
                up(a, q).wait_send()

            @pl.when((q >= z) & (z > 0))
            def _():
                down(a, q).wait_send()

            over_x(a, q).wait_send()
            to_mate(a, q, e, 0).wait_send()
            to_mate(a, q, across, 1).wait_send()
    gate_send(e, 0, across).wait_send()
    gate_send(e, 1, mate).wait_send()
    gate_send(across, 2, mate).wait_send()


def dispatched(tokens, grad_out, gates, pick, slots, w_gate, w_up, w_down):
    nz, ne = lax.axis_size("hid"), lax.axis_size("exp")
    tok, width = tokens.shape
    hidden = w_gate.shape[2]
    used = pick.shape[0]
    hbm = pl.BlockSpec(memory_space=pl.ANY)
    vmem = pl.BlockSpec(memory_space=pltpu.VMEM)
    bf16, f32 = jnp.bfloat16, jnp.float32
    dma = pltpu.SemaphoreType.DMA
    return pl.pallas_call(
        functools.partial(dispatch_kernel, nz, ne, tok, width),
        out_shape=(
            jax.ShapeDtypeStruct((used, hidden), bf16),
            jax.ShapeDtypeStruct((used, hidden), bf16),
            jax.ShapeDtypeStruct((used, 128), f32),
        ),
        in_specs=[hbm, hbm, hbm, vmem, vmem, hbm, hbm, hbm],
        out_specs=(vmem, vmem, vmem),
        scratch_shapes=[
            pltpu.VMEM((nz, ne, tok, width), bf16),
            pltpu.VMEM((nz, ne, tok, width), bf16),
            pltpu.VMEM((ne, tok, 128), bf16),
            pltpu.VMEM((2, width, hidden), bf16),
            pltpu.VMEM((2, width, hidden), bf16),
            pltpu.VMEM((2, hidden, width), bf16),
            pltpu.VMEM((used, hidden), f32),
            pltpu.VMEM((used, hidden), f32),
            pltpu.VMEM((used, hidden), f32),
            dma((2, nz)),
            dma((2, nz)),
            dma((2, nz)),
            dma((2, nz, 2)),
            dma((2, nz, ne)),
            dma((3,)),
            dma((ne,)),
            dma((2, 3)),
            dma((3,)),
        ],
        compiler_params=pltpu.CompilerParams(
            collective_id=0, has_side_effects=True, vmem_limit_bytes=56 * 1024 * 1024
        ),
        cost_estimate=pl.CostEstimate(
            flops=6 * used * hidden * width * nz,
            bytes_accessed=6 * hidden * width * nz,
            transcendentals=used * hidden,
        ),
        name="dispatch",
    )(tokens, grad_out, gates, pick, slots, w_gate, w_up, w_down)


def combine_kernel(nz, ne, tok, width, dpg_ref, dpu_ref, scat_ref, sd_ref, w1_ref, w3_ref, out_ref, gate_ref,
                   dense, cr, xs, xr, zs, zr, acc, w1, w3, scr, sxs, sxr, szs, szr,
                   css, crs, xss, xrs, zss, zrs, gcs, gcr, gxs, gxr, gzs, gzr, wsem):
    z = lax.axis_index("hid")
    e = lax.axis_index("exp")
    core = lax.rem(e, 2)
    mate = e + 1 - 2 * core
    mate_core = 1 - core
    across = lax.rem(e + 2, ne)
    x = e // 2
    far = 1 - x

    def weights(k, slot):
        q = lax.rem(z + 1 + k, nz)
        rows = pl.ds(pl.multiple_of(q * width, width), width)
        return (
            pltpu.make_async_copy(w1_ref.at[0, rows, :], w1.at[slot], wsem.at[slot, 0]),
            pltpu.make_async_copy(w3_ref.at[0, rows, :], w3.at[slot], wsem.at[slot, 1]),
        )

    def remote(src, dst, ssem, rsem, dev):
        return pltpu.make_async_remote_copy(
            src_ref=src, dst_ref=dst, send_sem=ssem, recv_sem=rsem, device_id=dev, device_id_type=MESH)

    def core_send(k, j):
        return remote(dense.at[k, mate_core + 2 * j], cr.at[k, j], css.at[k, j], crs.at[k, j], {"exp": mate})

    def x_send(k):
        return remote(xs.at[k], xr.at[k], xss.at[k], xrs.at[k], {"exp": across})

    def z_send(k):
        return remote(zs.at[k], zr.at[z], zss.at[k], zrs.at[z], {"hid": lax.rem(z + 1 + k, nz)})

    def gate_core(j):
        return remote(sd_ref.at[mate_core + 2 * j], scr.at[j], gcs.at[j], gcr.at[j], {"exp": mate})

    def gate_x():
        return remote(sxs, sxr, gxs.at[0], gxr.at[0], {"exp": across})

    def gate_z(k):
        return remote(szs, szr.at[z], gzs.at[k], gzr.at[z], {"hid": lax.rem(z + 1 + k, nz)})

    for k in range(2):
        for c in weights(k, k):
            c.start()

    barrier = pltpu.get_barrier_semaphore()
    pl.semaphore_signal(barrier, inc=1, device_id={"exp": mate}, device_id_type=MESH)
    pl.semaphore_signal(barrier, inc=1, device_id={"exp": across}, device_id_type=MESH)
    for k in range(nz - 1):
        pl.semaphore_signal(barrier, inc=1, device_id={"hid": lax.rem(z + 1 + k, nz)}, device_id_type=MESH)
    pl.semaphore_wait(barrier, nz + 1)

    for j in range(2):
        gate_core(j).start()

    def multiply(k):
        slot = lax.rem(k, 2)
        for c in weights(k, slot):
            c.wait()

        @pl.loop(0, width // 256)
        def _(t):
            rows = pl.ds(pl.multiple_of(t * 256, 256), 256)
            part = lax.dot_general(dpg_ref[...], w1[slot, rows, :], CONTRACT_LAST, preferred_element_type=jnp.float32)
            part += lax.dot_general(dpu_ref[...], w3[slot, rows, :], CONTRACT_LAST, preferred_element_type=jnp.float32)
            spread = jnp.dot(scat_ref[...], part.astype(jnp.bfloat16), preferred_element_type=jnp.float32)
            dense[k, :, :, rows] = spread.astype(jnp.bfloat16).reshape(ne, tok, 256)

        for j in range(2):
            core_send(k, j).start()

        @pl.when(k + 2 < nz)
        def _():
            for c in weights(k + 2, slot):
                c.start()

    def to_x(k):
        for j in range(2):
            core_send(k, j).wait_recv()
        both = dense[k, core + 2 * far].astype(jnp.float32) + cr[k, far].astype(jnp.float32)
        xs[k] = both.astype(jnp.bfloat16)
        x_send(k).start()

    def total(k):
        x_send(k).wait_recv()
        return (
            dense[k, e].astype(jnp.float32) + cr[k, x].astype(jnp.float32) + xr[k].astype(jnp.float32)
        )

    def to_z(k):
        zs[k] = total(k).astype(jnp.bfloat16)
        z_send(k).start()

    @pl.loop(0, nz)
    def _(k):
        multiply(k)
        to_x(k)

        @pl.when(k == 0)
        def _():
            for j in range(2):
                gate_core(j).wait_recv()
            sxs[...] = sd_ref[core + 2 * far] + scr[far]
            gate_x().start()

        @pl.when(k == 1)
        def _():
            gate_x().wait_recv()
            own_sum = sd_ref[e] + scr[x] + sxr[...]
            szs[...] = own_sum
            szr[z] = own_sum
            for i in range(nz - 1):
                gate_z(i).start()

        @pl.when(k >= 2)
        def _():
            to_z(k - 2)

    to_z(nz - 2)
    acc[...] = total(nz - 1)
    for k in range(nz - 1):
        source = lax.rem(z + 1 + k, nz)
        remote(zs.at[k], zr.at[source], zss.at[k], zrs.at[source], {"hid": source}).wait_recv()
        acc[...] += zr[source].astype(jnp.float32)
        remote(szs, szr.at[source], gzs.at[k], gzr.at[source], {"hid": source}).wait_recv()
    out_ref[...] = acc[...].astype(jnp.bfloat16)
    gate_total = szr[0]
    for q in range(1, nz):
        gate_total += szr[q]
    gate_ref[...] = gate_total

    for j in range(2):
        gate_core(j).wait_send()
    gate_x().wait_send()
    for k in range(nz):
        for j in range(2):
            core_send(k, j).wait_send()
        x_send(k).wait_send()
        if k < nz - 1:
            z_send(k).wait_send()
            gate_z(k).wait_send()


def returned(d_pre_gate, d_pre_up, scatter, score_dense, w_gate, w_up, tok, width):
    nz, ne = lax.axis_size("hid"), lax.axis_size("exp")
    used, hidden = d_pre_gate.shape
    hbm = pl.BlockSpec(memory_space=pl.ANY)
    vmem = pl.BlockSpec(memory_space=pltpu.VMEM)
    bf16, f32 = jnp.bfloat16, jnp.float32
    dma = pltpu.SemaphoreType.DMA
    return pl.pallas_call(
        functools.partial(combine_kernel, nz, ne, tok, width),
        out_shape=(
            jax.ShapeDtypeStruct((tok, width), bf16),
            jax.ShapeDtypeStruct((8, tok), f32),
        ),
        in_specs=[vmem, vmem, vmem, vmem, hbm, hbm],
        out_specs=(vmem, vmem),
        scratch_shapes=[
            pltpu.VMEM((nz, ne, tok, width), bf16),
            pltpu.VMEM((nz, 2, tok, width), bf16),
            pltpu.VMEM((nz, tok, width), bf16),
            pltpu.VMEM((nz, tok, width), bf16),
            pltpu.VMEM((nz, tok, width), bf16),
            pltpu.VMEM((nz, tok, width), bf16),
            pltpu.VMEM((tok, width), f32),
            pltpu.VMEM((2, width, hidden), bf16),
            pltpu.VMEM((2, width, hidden), bf16),
            pltpu.VMEM((2, 8, tok), f32),
            pltpu.VMEM((8, tok), f32),
            pltpu.VMEM((8, tok), f32),
            pltpu.VMEM((8, tok), f32),
            pltpu.VMEM((nz, 8, tok), f32),
            dma((nz, 2)),
            dma((nz, 2)),
            dma((nz,)),
            dma((nz,)),
            dma((nz,)),
            dma((nz,)),
            dma((2,)),
            dma((2,)),
            dma((1,)),
            dma((1,)),
            dma((nz,)),
            dma((nz,)),
            dma((2, 2)),
        ],
        compiler_params=pltpu.CompilerParams(
            collective_id=1, has_side_effects=True, vmem_limit_bytes=52 * 1024 * 1024
        ),
        cost_estimate=pl.CostEstimate(
            flops=4 * used * hidden * width * nz,
            bytes_accessed=4 * hidden * width * nz,
            transcendentals=0,
        ),
        name="combine",
    )(d_pre_gate, d_pre_up, scatter, score_dense, w_gate, w_up)


def fast_local(tokens, grad_out, gates, block_experts, w_gate, w_up, w_down):
    n_experts = lax.axis_size("exp")
    own_index = lax.axis_index("exp")
    tok_dev, width_dev = tokens.shape
    blocks_all = block_experts.shape[0]
    per_home = tok_dev // BLOCK
    capacity = blocks_all // 2
    used_count = capacity * BLOCK
    list_block, list_slot, live = routing(block_experts, own_index)
    slot_hot = (list_slot[:, None] == jnp.arange(2, dtype=jnp.int32)[None, :]).astype(jnp.float32)
    slot_hot = slot_hot * live[:, None].astype(jnp.float32)
    row = jnp.where(live, list_block * BLOCK, -used_count * n_experts)[:, None] + jnp.arange(BLOCK, dtype=jnp.int32)[None, :]
    row = row.reshape(used_count, 1)
    pick = (row == jnp.arange(blocks_all * BLOCK, dtype=jnp.int32)[None, :]).astype(jnp.bfloat16)
    lane = jnp.arange(128, dtype=jnp.int32)[None, None, :]
    slots = ((list_slot[:, None, None] == lane) & live[:, None, None]).astype(jnp.float32)
    slots = jnp.broadcast_to(slots, (capacity, BLOCK, 128)).reshape(used_count, 128)
    gates_wide = jnp.pad(gates, ((0, 0), (0, 126)))
    d_pre_gate, d_pre_up, score_lanes = dispatched(
        tokens, grad_out, gates_wide, pick, slots, w_gate, w_up, w_down
    )
    score = jnp.sum(score_lanes, axis=1).reshape(capacity, BLOCK)
    homes = jnp.arange(blocks_all, dtype=jnp.int32)
    goes = (list_block[:, None] == homes[None, :]).astype(jnp.float32)[:, :, None] * slot_hot[:, None, :]
    goes = jnp.pad(goes, ((0, 0), (0, 0), (0, 6)))
    score_dense = jnp.sum(goes[:, :, :, None] * score[:, None, None, :], axis=0)
    grad, gate_rows = returned(
        d_pre_gate, d_pre_up, pick.T, score_dense, w_gate, w_up, tok_dev, width_dev
    )
    return grad, gate_rows[:2].T


def combined(owned, score, list_block, live, slot_hot, tok_dev, width_dev, capacity):
    n_experts = lax.axis_size("exp")
    own_index = lax.axis_index("exp")
    per_home = tok_dev // BLOCK
    result_cols = owned.reshape(width_dev, capacity, BLOCK)
    score_blocks = score.reshape(capacity, BLOCK)

    def share(home):
        wanted = home * per_home + jnp.arange(per_home, dtype=jnp.int32)
        select = ((list_block[None, :] == wanted[:, None]) & live[None, :]).astype(jnp.float32)
        grad_part = jnp.einsum("bi,dir->dbr", select, result_cols, precision=HIGHEST).reshape(
            width_dev, tok_dev
        )
        gate_part = jnp.einsum(
            "bi,ik,ir->kbr", select, slot_hot, score_blocks, precision=HIGHEST
        ).reshape(2, tok_dev)
        return (grad_part, gate_part)

    zero_totals = (
        jnp.zeros((width_dev, tok_dev), jnp.float32),
        jnp.zeros((2, tok_dev), jnp.float32),
    )

    def single_turn(step, totals):
        grad_part, gate_part = share((own_index + 1 + step) % n_experts)
        return passed_along((totals[0] + grad_part, totals[1] + gate_part), "exp", -1)

    totals = lax.fori_loop(0, n_experts - 1, single_turn, zero_totals)
    grad_part, gate_part = share(own_index)
    grad_total = totals[0] + grad_part
    gate_total = totals[1] + gate_part
    return (grad_total.T.astype(jnp.bfloat16), gate_total.T)


def local(tokens, grad_out, gates, block_experts, w_gate, w_up, w_down):
    own_index = lax.axis_index("exp")
    tok_dev, width_dev = tokens.shape
    blocks_all = block_experts.shape[0]
    capacity = blocks_all // 2
    used_count = capacity * BLOCK
    list_block, list_slot, live = routing(block_experts, own_index)
    row_index = (list_block[:, None] * BLOCK + jnp.arange(BLOCK, dtype=jnp.int32)[None, :]).reshape(
        used_count
    )
    x_home, dy_home, gate_home = (
        lax.all_gather(tokens, "exp", axis=0, tiled=True),
        lax.all_gather(grad_out, "exp", axis=0, tiled=True),
        lax.all_gather(gates, "exp", axis=0, tiled=True),
    )
    gate_pick = (
        jnp.take(gate_home, row_index, axis=0).astype(jnp.float32).reshape(capacity, BLOCK, 2)
    )
    slot_hot = (list_slot[:, None] == jnp.arange(2, dtype=jnp.int32)[None, :]).astype(jnp.float32)
    slot_hot = slot_hot * live[:, None].astype(jnp.float32)
    gate_column = jnp.sum(gate_pick * slot_hot[:, None, :], axis=2).reshape(used_count)
    x_piece = jnp.take(lax.all_gather(x_home, "hid", axis=1, tiled=True), row_index, axis=0)
    dy_piece = jnp.take(lax.all_gather(dy_home, "hid", axis=1, tiled=True), row_index, axis=0)
    pre_gate = jnp.dot(x_piece, w_gate[0], preferred_element_type=jnp.float32)
    pre_up = jnp.dot(x_piece, w_up[0], preferred_element_type=jnp.float32)
    d_hidden = lax.dot_general(dy_piece, w_down[0], CONTRACT_LAST, preferred_element_type=jnp.float32)
    sigmoid_gate = jax.nn.sigmoid(pre_gate)
    activated = pre_gate * sigmoid_gate
    score_part = jnp.sum(activated * pre_up * d_hidden, axis=1)
    score = lax.psum(score_part, "hid")
    scaled = gate_column[:, None] * d_hidden
    d_pre_gate = (scaled * pre_up * sigmoid_gate * (1.0 + pre_gate * (1.0 - sigmoid_gate))).astype(
        jnp.bfloat16
    )
    d_pre_up = (scaled * activated).astype(jnp.bfloat16)
    first = lax.dot_general(w_gate[0], d_pre_gate, CONTRACT_LAST, preferred_element_type=jnp.float32)
    owned = lax.psum_scatter(
        first
        + lax.dot_general(w_up[0], d_pre_up, CONTRACT_LAST, preferred_element_type=jnp.float32),
        "hid",
        scatter_dimension=0,
        tiled=True,
    )
    return combined(owned, score, list_block, live, slot_hot, tok_dev, width_dev, capacity)


def solution(mesh):
    placed = (
        P(("grp", "exp"), "hid"),
        P(("grp", "exp"), "hid"),
        P(("grp", "exp"), None),
        P("grp", None),
        P("exp", None, "hid"),
        P("exp", None, "hid"),
        P("exp", "hid", None),
    )
    body = fast_local if (mesh.shape["exp"], mesh.shape["hid"]) == (4, 4) else local
    return jax.shard_map(
        body,
        mesh=mesh,
        in_specs=placed,
        out_specs=(P(("grp", "exp"), "hid"), P(("grp", "exp"), None)),
        check_vma=False,
    )
```

```python
import functools
import jax
import jax.numpy as jnp
from jax import lax
from jax.experimental import pallas as pl
from jax.experimental.pallas import tpu as pltpu
from jax.sharding import PartitionSpec as P

BLOCK = 128


HIGHEST = lax.Precision.HIGHEST
CONTRACT_LAST = (((1,), (1,)), ((), ()))
MESH = pl.DeviceIdType.MESH
TILE = 512


def passed_along(block, axis, distance):
    devices = range(lax.axis_size(axis))
    route = [((i - distance) % len(devices), i) for i in devices]
    return lax.ppermute(block, axis, route)


def routing(block_experts, own_index):
    blocks_all = block_experts.shape[0]
    capacity = blocks_all // 2
    matched = block_experts == own_index
    chosen = jnp.any(matched, axis=1)
    slot_of = matched[:, 1].astype(jnp.int32)
    position = jnp.cumsum(chosen.astype(jnp.int32)) - 1
    placed = (position[None, :] == jnp.arange(capacity, dtype=jnp.int32)[:, None]) & chosen[None, :]
    placed_int = placed.astype(jnp.int32)
    list_block = jnp.sum(placed_int * jnp.arange(blocks_all, dtype=jnp.int32)[None, :], axis=1)
    list_slot = jnp.sum(placed_int * slot_of[None, :], axis=1)
    live = jnp.any(placed, axis=1)
    return list_block, list_slot, live


def layer_kernel(nz, ne, tok, width, tok_ref, dy_ref, gate_ref, pick_ref, slot_ref, home_ref, scat_ref,
                 w1_ref, w3_ref, w2_ref, out_ref, grad_gate_ref,
                 xb, db, gb, w1, w3, w2, pg, pu, dh, dpg_ref, dpu_ref, score_ref, sd_ref,
                 dense, cr, xs, xr, zs, zr, acc, scr, sxs, sxr, szs, szr,
                 s_up, s_dn, s_x, s_c, rsem, gs, gr, wsem, lsem,
                 css, crs, xss, xrs, zss, zrs, gcs, gcr, gxs, gxr, gzs, gzr):
    z = lax.axis_index("hid")
    e = lax.axis_index("exp")
    mate = e + 1 - 2 * lax.rem(e, 2)
    across = lax.rem(e + 2, ne)
    bufs = (xb, db)
    hidden = w1.shape[2]

    def weights(q, slot):
        rows = pl.ds(pl.multiple_of(q * width, width), width)
        return (
            pltpu.make_async_copy(w1_ref.at[0, rows, :], w1.at[slot], wsem.at[slot, 0]),
            pltpu.make_async_copy(w3_ref.at[0, rows, :], w3.at[slot], wsem.at[slot, 1]),
            pltpu.make_async_copy(w2_ref.at[0, :, rows], w2.at[slot], wsem.at[slot, 2]),
        )

    def send(a, zq, eq, ssem, dev):
        return pltpu.make_async_remote_copy(
            src_ref=bufs[a].at[zq, eq], dst_ref=bufs[a].at[zq, eq],
            send_sem=ssem, recv_sem=rsem.at[a, zq, eq],
            device_id=dev, device_id_type=MESH)

    def up(a, zq):
        return send(a, zq, e, s_up.at[a, zq], {"hid": z + 1})

    def down(a, zq):
        return send(a, zq, e, s_dn.at[a, zq], {"hid": z - 1})

    def over_x(a, zq):
        return send(a, zq, e, s_x.at[a, zq], {"exp": across})

    def to_mate(a, zq, eq, k):
        return send(a, zq, eq, s_c.at[a, zq, k], {"exp": mate})

    def arrived(a, zq, eq):
        send(a, zq, eq, s_x.at[a, zq], {"exp": across}).wait_recv()

    def gate_send(eq, k, dev):
        return pltpu.make_async_remote_copy(
            src_ref=gb.at[eq], dst_ref=gb.at[eq], send_sem=gs.at[k], recv_sem=gr.at[eq],
            device_id={"exp": dev}, device_id_type=MESH)

    own = (
        pltpu.make_async_copy(tok_ref, xb.at[z, e], lsem.at[0]),
        pltpu.make_async_copy(dy_ref, db.at[z, e], lsem.at[1]),
        pltpu.make_async_copy(gate_ref, gb.at[e], lsem.at[2]),
    )
    for c in own:
        c.start()
    for c in weights(z, 1):
        c.start()

    @pl.when(z > 0)
    def _():
        for c in weights(z - 1, 0):
            c.start()

    barrier = pltpu.get_barrier_semaphore()
    pl.semaphore_signal(barrier, inc=1, device_id={"exp": mate}, device_id_type=MESH)
    pl.semaphore_signal(barrier, inc=1, device_id={"exp": across}, device_id_type=MESH)

    for k in range(nz - 1):
        pl.semaphore_signal(barrier, inc=1, device_id={"hid": lax.rem(z + 1 + k, nz)}, device_id_type=MESH)
    pl.semaphore_wait(barrier, nz + 1)

    for c in own:
        c.wait()
    for a in range(2):
        @pl.when(z < nz - 1)
        def _():
            up(a, z).start()

        @pl.when(z > 0)
        def _():
            down(a, z).start()

        over_x(a, z).start()
        to_mate(a, z, e, 0).start()
    gate_send(e, 0, across).start()
    gate_send(e, 1, mate).start()

    pg[...] = jnp.zeros_like(pg)
    pu[...] = jnp.zeros_like(pu)
    dh[...] = jnp.zeros_like(dh)

    def pass_on(d):
        for a in range(2):
            @pl.when(z - d >= 0)
            def _():
                arrived(a, z - d, e)

                @pl.when(z < nz - 1)
                def _():
                    up(a, z - d).start()

                over_x(a, z - d).start()
                to_mate(a, z - d, e, 0).start()

            @pl.when(z + d < nz)
            def _():
                arrived(a, z + d, e)

                @pl.when(z > 0)
                def _():
                    down(a, z + d).start()

                over_x(a, z + d).start()
                to_mate(a, z + d, e, 0).start()

    mate_across = lax.rem(mate + 2, ne)

    def picked(a, zq):
        arrived(a, zq, across)
        to_mate(a, zq, across, 1).start()
        arrived(a, zq, mate)
        arrived(a, zq, mate_across)
        rows = bufs[a][zq].reshape(ne * tok, width)
        return jnp.dot(pick_ref[...], rows, preferred_element_type=jnp.float32).astype(jnp.bfloat16)

    def compute(zq, slot):
        pending = weights(zq, slot)
        xs = picked(0, zq)
        pending[0].wait()
        pending[1].wait()

        @pl.loop(0, hidden // TILE)
        def _(t):
            cols = pl.ds(pl.multiple_of(t * TILE, TILE), TILE)
            pg[:, cols] += jnp.dot(xs, w1[slot, :, cols], preferred_element_type=jnp.float32)
            pu[:, cols] += jnp.dot(xs, w3[slot, :, cols], preferred_element_type=jnp.float32)

        ds = picked(1, zq)
        pending[2].wait()

        @pl.loop(0, hidden // TILE)
        def _(t):
            cols = pl.ds(pl.multiple_of(t * TILE, TILE), TILE)
            dh[:, cols] += lax.dot_general(ds, w2[slot, cols, :], CONTRACT_LAST, preferred_element_type=jnp.float32)

    @pl.loop(0, nz)
    def _(d):
        @pl.when(d < nz - 1)
        def _():
            pass_on(d + 1)

        @pl.when((d > 0) & (z - d >= 0))
        def _():
            compute(z - d, 0)

            @pl.when(z - d - 1 >= 0)
            def _():
                for c in weights(z - d - 1, 0):
                    c.start()

        @pl.when(z + d < nz)
        def _():
            compute(z + d, 1)

            @pl.when(z + d + 1 < nz)
            def _():
                for c in weights(z + d + 1, 1):
                    c.start()

    core = lax.rem(e, 2)
    mate_core = 1 - core
    x = e // 2
    far = 1 - x

    def again(k, slot):
        q = lax.rem(z + 1 + k, nz)
        rows = pl.ds(pl.multiple_of(q * width, width), width)
        return (
            pltpu.make_async_copy(w1_ref.at[0, rows, :], w1.at[slot], wsem.at[slot, 0]),
            pltpu.make_async_copy(w3_ref.at[0, rows, :], w3.at[slot], wsem.at[slot, 1]),
        )

    def remote(src, dst, ssem, rsem, dev):
        return pltpu.make_async_remote_copy(
            src_ref=src, dst_ref=dst, send_sem=ssem, recv_sem=rsem, device_id=dev, device_id_type=MESH)

    def core_send(k, j):
        return remote(dense.at[k, mate_core + 2 * j], cr.at[k, j], css.at[k, j], crs.at[k, j], {"exp": mate})

    def x_send(k):
        return remote(xs.at[k], xr.at[k], xss.at[k], xrs.at[k], {"exp": across})

    def z_send(k):
        return remote(zs.at[k], zr.at[z], zss.at[k], zrs.at[z], {"hid": lax.rem(z + 1 + k, nz)})

    def gate_core(j):
        return remote(sd_ref.at[mate_core + 2 * j], scr.at[j], gcs.at[j], gcr.at[j], {"exp": mate})

    def gate_x():
        return remote(sxs, sxr, gxs.at[0], gxr.at[0], {"exp": across})

    def gate_z(k):
        return remote(szs, szr.at[z], gzs.at[k], gzr.at[z], {"hid": lax.rem(z + 1 + k, nz)})

    for k in range(2):
        for c in again(k, k):
            c.start()

    gate_send(across, 2, across).wait_recv()
    gate_send(across, 2, mate).start()
    gate_send(mate, 2, mate).wait_recv()
    gate_send(lax.rem(mate + 2, ne), 2, mate).wait_recv()
    gates = jnp.dot(pick_ref[...], gb[...].reshape(ne * tok, gb.shape[2]), preferred_element_type=jnp.float32)
    gate = jnp.sum(gates * slot_ref[...], axis=1, keepdims=True)
    score_ref[...] = jnp.zeros_like(score_ref)

    @pl.loop(0, hidden // 128)
    def _(t):
        cols = pl.ds(pl.multiple_of(t * 128, 128), 128)
        g = pg[:, cols]
        u = pu[:, cols]
        h = dh[:, cols]
        sig = 1.0 / (1.0 + jnp.exp(-g))
        act = g * sig
        score_ref[...] += act * u * h
        scaled = gate * h
        dpg_ref[:, cols] = (scaled * u * sig * (1.0 + g * (1.0 - sig))).astype(jnp.bfloat16)
        dpu_ref[:, cols] = (scaled * act).astype(jnp.bfloat16)

    score = jnp.sum(score_ref[...], axis=1, keepdims=True) * slot_ref[...]
    for home in range(ne):
        mine = score * home_ref[:, home : home + 1]
        placed = mine[:tok]
        for i in range(1, mine.shape[0] // tok):
            placed += mine[i * tok : (i + 1) * tok]
        sd_ref[home] = placed

    for j in range(2):
        gate_core(j).start()

    def multiply(k):
        slot = lax.rem(k, 2)
        for c in again(k, slot):
            c.wait()

        @pl.loop(0, width // 256)
        def _(t):
            rows = pl.ds(pl.multiple_of(t * 256, 256), 256)
            part = lax.dot_general(dpg_ref[...], w1[slot, rows, :], CONTRACT_LAST, preferred_element_type=jnp.float32)
            part += lax.dot_general(dpu_ref[...], w3[slot, rows, :], CONTRACT_LAST, preferred_element_type=jnp.float32)
            spread = jnp.dot(scat_ref[...], part.astype(jnp.bfloat16), preferred_element_type=jnp.float32)
            dense[k, :, :, rows] = spread.astype(jnp.bfloat16).reshape(ne, tok, 256)

        for j in range(2):
            core_send(k, j).start()

        @pl.when(k + 2 < nz)
        def _():
            for c in again(k + 2, slot):
                c.start()

    def to_x(k):
        for j in range(2):
            core_send(k, j).wait_recv()
        both = dense[k, core + 2 * far].astype(jnp.float32) + cr[k, far].astype(jnp.float32)
        xs[k] = both.astype(jnp.bfloat16)
        x_send(k).start()

    def total(k):
        x_send(k).wait_recv()
        return (
            dense[k, e].astype(jnp.float32) + cr[k, x].astype(jnp.float32) + xr[k].astype(jnp.float32)
        )

    def to_z(k):
        zs[k] = total(k).astype(jnp.bfloat16)
        z_send(k).start()

    @pl.loop(0, nz)
    def _(k):
        multiply(k)
        to_x(k)

        @pl.when(k == 0)
        def _():
            for j in range(2):
                gate_core(j).wait_recv()
            sxs[...] = sd_ref[core + 2 * far] + scr[far]
            gate_x().start()

        @pl.when(k == 1)
        def _():
            gate_x().wait_recv()
            own_sum = sd_ref[e] + scr[x] + sxr[...]
            szs[...] = own_sum
            szr[z] = own_sum
            for i in range(nz - 1):
                gate_z(i).start()

        @pl.when(k >= 2)
        def _():
            to_z(k - 2)

    to_z(nz - 2)
    acc[...] = total(nz - 1)
    for k in range(nz - 1):
        source = lax.rem(z + 1 + k, nz)
        remote(zs.at[k], zr.at[source], zss.at[k], zrs.at[source], {"hid": source}).wait_recv()
        acc[...] += zr[source].astype(jnp.float32)
        remote(szs, szr.at[source], gzs.at[k], gzr.at[source], {"hid": source}).wait_recv()
    out_ref[...] = acc[...].astype(jnp.bfloat16)
    gate_total = szr[0]
    for q in range(1, nz):
        gate_total += szr[q]
    grad_gate_ref[...] = gate_total

    for j in range(2):
        gate_core(j).wait_send()
    gate_x().wait_send()
    for k in range(nz):
        for j in range(2):
            core_send(k, j).wait_send()
        x_send(k).wait_send()
        if k < nz - 1:
            z_send(k).wait_send()
            gate_z(k).wait_send()

    @pl.loop(0, nz)
    def _(q):
        for a in range(2):
            @pl.when((q <= z) & (z < nz - 1))
            def _():
                up(a, q).wait_send()

            @pl.when((q >= z) & (z > 0))
            def _():
                down(a, q).wait_send()

            over_x(a, q).wait_send()
            to_mate(a, q, e, 0).wait_send()
            to_mate(a, q, across, 1).wait_send()
    gate_send(e, 0, across).wait_send()
    gate_send(e, 1, mate).wait_send()
    gate_send(across, 2, mate).wait_send()


def layer(tokens, grad_out, gates, pick, slots, homes, w_gate, w_up, w_down):
    nz, ne = lax.axis_size("hid"), lax.axis_size("exp")
    tok, width = tokens.shape
    hidden = w_gate.shape[2]
    used = pick.shape[0]
    hbm = pl.BlockSpec(memory_space=pl.ANY)
    vmem = pl.BlockSpec(memory_space=pltpu.VMEM)
    bf16, f32 = jnp.bfloat16, jnp.float32
    dma = pltpu.SemaphoreType.DMA
    return pl.pallas_call(
        functools.partial(layer_kernel, nz, ne, tok, width),
        out_shape=(
            jax.ShapeDtypeStruct((tok, width), bf16),
            jax.ShapeDtypeStruct((tok, 128), f32),
        ),
        in_specs=[hbm, hbm, hbm, vmem, vmem, vmem, vmem, hbm, hbm, hbm],
        out_specs=(vmem, vmem),
        scratch_shapes=[
            pltpu.VMEM((nz, ne, tok, width), bf16),
            pltpu.VMEM((nz, ne, tok, width), bf16),
            pltpu.VMEM((ne, tok, 128), bf16),
            pltpu.VMEM((2, width, hidden), bf16),
            pltpu.VMEM((2, width, hidden), bf16),
            pltpu.VMEM((2, hidden, width), bf16),
            pltpu.VMEM((used, hidden), f32),
            pltpu.VMEM((used, hidden), f32),
            pltpu.VMEM((used, hidden), f32),
            pltpu.VMEM((used, hidden), bf16),
            pltpu.VMEM((used, hidden), bf16),
            pltpu.VMEM((used, 128), f32),
            pltpu.VMEM((ne, tok, 128), f32),
            pltpu.VMEM((nz, ne, tok, width), bf16),
            pltpu.VMEM((nz, 2, tok, width), bf16),
            pltpu.VMEM((nz, tok, width), bf16),
            pltpu.VMEM((nz, tok, width), bf16),
            pltpu.VMEM((nz, tok, width), bf16),
            pltpu.VMEM((nz, tok, width), bf16),
            pltpu.VMEM((tok, width), f32),
            pltpu.VMEM((2, tok, 128), f32),
            pltpu.VMEM((tok, 128), f32),
            pltpu.VMEM((tok, 128), f32),
            pltpu.VMEM((tok, 128), f32),
            pltpu.VMEM((nz, tok, 128), f32),
            dma((2, nz)),
            dma((2, nz)),
            dma((2, nz)),
            dma((2, nz, 2)),
            dma((2, nz, ne)),
            dma((3,)),
            dma((ne,)),
            dma((2, 3)),
            dma((3,)),
            dma((nz, 2)),
            dma((nz, 2)),
            dma((nz,)),
            dma((nz,)),
            dma((nz,)),
            dma((nz,)),
            dma((2,)),
            dma((2,)),
            dma((1,)),
            dma((1,)),
            dma((nz,)),
            dma((nz,)),
        ],
        compiler_params=pltpu.CompilerParams(
            collective_id=0, has_side_effects=True, vmem_limit_bytes=60 * 1024 * 1024
        ),
        name="layer",
    )(tokens, grad_out, gates, pick, slots, homes, pick.T, w_gate, w_up, w_down)


def fast_local(tokens, grad_out, gates, block_experts, w_gate, w_up, w_down):
    n_experts = lax.axis_size("exp")
    own_index = lax.axis_index("exp")
    tok_dev, width_dev = tokens.shape
    blocks_all = block_experts.shape[0]
    per_home = tok_dev // BLOCK
    capacity = blocks_all // 2
    used_count = capacity * BLOCK
    list_block, list_slot, live = routing(block_experts, own_index)
    slot_hot = (list_slot[:, None] == jnp.arange(2, dtype=jnp.int32)[None, :]).astype(jnp.float32)
    slot_hot = slot_hot * live[:, None].astype(jnp.float32)
    row = jnp.where(live, list_block * BLOCK, -used_count * n_experts)[:, None] + jnp.arange(BLOCK, dtype=jnp.int32)[None, :]
    row = row.reshape(used_count, 1)
    pick = (row == jnp.arange(blocks_all * BLOCK, dtype=jnp.int32)[None, :]).astype(jnp.bfloat16)
    lane = jnp.arange(128, dtype=jnp.int32)[None, None, :]
    slots = ((list_slot[:, None, None] == lane) & live[:, None, None]).astype(jnp.float32)
    slots = jnp.broadcast_to(slots, (capacity, BLOCK, 128)).reshape(used_count, 128)
    gates_wide = jnp.pad(gates, ((0, 0), (0, 126)))
    homes = ((list_block[:, None, None] == lane) & live[:, None, None]).astype(jnp.float32)
    homes = jnp.broadcast_to(homes, (capacity, BLOCK, 128)).reshape(used_count, 128)
    grad, gate_lanes = layer(tokens, grad_out, gates_wide, pick, slots, homes, w_gate, w_up, w_down)
    return grad, gate_lanes[:, :2]


def combined(owned, score, list_block, live, slot_hot, tok_dev, width_dev, capacity):
    n_experts = lax.axis_size("exp")
    own_index = lax.axis_index("exp")
    per_home = tok_dev // BLOCK
    result_cols = owned.reshape(width_dev, capacity, BLOCK)
    score_blocks = score.reshape(capacity, BLOCK)

    def share(home):
        wanted = home * per_home + jnp.arange(per_home, dtype=jnp.int32)
        select = ((list_block[None, :] == wanted[:, None]) & live[None, :]).astype(jnp.float32)
        grad_part = jnp.einsum("bi,dir->dbr", select, result_cols, precision=HIGHEST).reshape(
            width_dev, tok_dev
        )
        gate_part = jnp.einsum(
            "bi,ik,ir->kbr", select, slot_hot, score_blocks, precision=HIGHEST
        ).reshape(2, tok_dev)
        return (grad_part, gate_part)

    zero_totals = (
        jnp.zeros((width_dev, tok_dev), jnp.float32),
        jnp.zeros((2, tok_dev), jnp.float32),
    )

    def single_turn(step, totals):
        grad_part, gate_part = share((own_index + 1 + step) % n_experts)
        return passed_along((totals[0] + grad_part, totals[1] + gate_part), "exp", -1)

    totals = lax.fori_loop(0, n_experts - 1, single_turn, zero_totals)
    grad_part, gate_part = share(own_index)
    grad_total = totals[0] + grad_part
    gate_total = totals[1] + gate_part
    return (grad_total.T.astype(jnp.bfloat16), gate_total.T)


def local(tokens, grad_out, gates, block_experts, w_gate, w_up, w_down):
    own_index = lax.axis_index("exp")
    tok_dev, width_dev = tokens.shape
    blocks_all = block_experts.shape[0]
    capacity = blocks_all // 2
    used_count = capacity * BLOCK
    list_block, list_slot, live = routing(block_experts, own_index)
    row_index = (list_block[:, None] * BLOCK + jnp.arange(BLOCK, dtype=jnp.int32)[None, :]).reshape(
        used_count
    )
    x_home, dy_home, gate_home = (
        lax.all_gather(tokens, "exp", axis=0, tiled=True),
        lax.all_gather(grad_out, "exp", axis=0, tiled=True),
        lax.all_gather(gates, "exp", axis=0, tiled=True),
    )
    gate_pick = (
        jnp.take(gate_home, row_index, axis=0).astype(jnp.float32).reshape(capacity, BLOCK, 2)
    )
    slot_hot = (list_slot[:, None] == jnp.arange(2, dtype=jnp.int32)[None, :]).astype(jnp.float32)
    slot_hot = slot_hot * live[:, None].astype(jnp.float32)
    gate_column = jnp.sum(gate_pick * slot_hot[:, None, :], axis=2).reshape(used_count)
    x_piece = jnp.take(lax.all_gather(x_home, "hid", axis=1, tiled=True), row_index, axis=0)
    dy_piece = jnp.take(lax.all_gather(dy_home, "hid", axis=1, tiled=True), row_index, axis=0)
    pre_gate = jnp.dot(x_piece, w_gate[0], preferred_element_type=jnp.float32)
    pre_up = jnp.dot(x_piece, w_up[0], preferred_element_type=jnp.float32)
    d_hidden = lax.dot_general(dy_piece, w_down[0], CONTRACT_LAST, preferred_element_type=jnp.float32)
    sigmoid_gate = jax.nn.sigmoid(pre_gate)
    activated = pre_gate * sigmoid_gate
    score_part = jnp.sum(activated * pre_up * d_hidden, axis=1)
    score = lax.psum(score_part, "hid")
    scaled = gate_column[:, None] * d_hidden
    d_pre_gate = (scaled * pre_up * sigmoid_gate * (1.0 + pre_gate * (1.0 - sigmoid_gate))).astype(
        jnp.bfloat16
    )
    d_pre_up = (scaled * activated).astype(jnp.bfloat16)
    first = lax.dot_general(w_gate[0], d_pre_gate, CONTRACT_LAST, preferred_element_type=jnp.float32)
    owned = lax.psum_scatter(
        first
        + lax.dot_general(w_up[0], d_pre_up, CONTRACT_LAST, preferred_element_type=jnp.float32),
        "hid",
        scatter_dimension=0,
        tiled=True,
    )
    return combined(owned, score, list_block, live, slot_hot, tok_dev, width_dev, capacity)


def solution(mesh):
    placed = (
        P(("grp", "exp"), "hid"),
        P(("grp", "exp"), "hid"),
        P(("grp", "exp"), None),
        P("grp", None),
        P("exp", None, "hid"),
        P("exp", None, "hid"),
        P("exp", "hid", None),
    )
    body = fast_local if (mesh.shape["exp"], mesh.shape["hid"]) == (4, 4) else local
    return jax.shard_map(
        body,
        mesh=mesh,
        in_specs=placed,
        out_specs=(P(("grp", "exp"), "hid"), P(("grp", "exp"), None)),
        check_vma=False,
    )
```
